512 devices in a mesh: grp: 16 (over z, core), tile: 32 (over y, x).
Axes of the slice: x: 4, y: 8, z: 8, core: 2. Of those that a mesh axis runs over, the one named last changes fastest.
Arguments:
- tracer_adjoint: float32 [2, 96, 128, 4096], P(None, 'tile', 'grp'), may hold values from -6 to 6
- surface_adjoint: float32 [128, 4096], P('grp', 'tile'), may hold values from -6 to 6
- velocity: bfloat16 [2, 96, 128, 4096], P(None, 'tile', 'grp'), may hold values from -0.5 to 0.5
- vertical_coupling: float32 [96, 128, 4096], P(None, 'grp', 'tile'), may hold values from 0.05 to 3000, as said below
- ocean_levels: int32 [128, 4096], P('grp', 'tile'), may hold values from 0 to 96, as said below
- face_conductance: float32 [4, 128, 4096], P(None, 'grp', 'tile'), may hold values from 0.5 to 8, as said below
- buoyancy_weights: float32 [2, 96], replicated, may hold values from -1 to 1
- surface_flux: float32 [2], replicated, may hold values from 0.5 to 2
Outputs:
- tracer_result: float32 [2, 96, 128, 4096], P(None, 'tile', 'grp')
- surface_result: float32 [128, 4096], P('grp', 'tile')
The draws below stay inside these ranges and needn't reach their ends.
Inputs may be any that keep to these rules, and one draw needn't show every extreme that they name: The faces agree between cells: face_conductance[1] of a cell equals face_conductance[0] of the cell to its west, and face_conductance[3] equals face_conductance[2] of the cell to its south, where such cells exist. `vertical_coupling`: mixing coefficients are positive. `ocean_levels`: wet levels of a column, from land to the full depth of 96 levels.
All inputs are finite; a program needn't handle non-finite values.
Results may differ from the reference program's by a relative error of at most 0.0003.
Values may be sent and summed in bfloat16 or wider, within the bound.
A program may use at most 64 MiB of HBM per device.

```python
import math
import jax
import jax.numpy as jnp
from jax import lax

NZ = 96
SOLVE_ITERS = 12
STEPS = 2
ROWS = 128
NX = 4096


def draw_face_conductance(key, part):
    first, second, third, fourth = jax.random.split(key, 4)
    low_end = math.log(0.5)
    high_end = math.log(4.0)
    eastern = jnp.exp(jax.random.uniform(first, (ROWS, NX), jnp.float32, low_end, high_end))
    northern = jnp.exp(jax.random.uniform(second, (ROWS, NX), jnp.float32, low_end, high_end))
    west_edge = jnp.exp(jax.random.uniform(third, (ROWS, 1), jnp.float32, low_end, high_end))
    south_edge = jnp.exp(jax.random.uniform(fourth, (1, NX), jnp.float32, low_end, high_end))
    western = jnp.concatenate([west_edge, eastern[:, :-1]], axis=1)
    southern = jnp.concatenate([south_edge, northern[:-1]], axis=0)
    return jnp.stack([eastern, western, northern, southern]).astype(jnp.float32)


def draw_vertical_coupling(key, part):
    first, second, third = jax.random.split(jax.random.fold_in(key, 71), 3)
    base = jnp.exp(jax.random.uniform(first, (NZ, ROWS, NX), jnp.float32, math.log(0.05), math.log(20.0)))
    strong_low = math.log(100.0)
    strong_high = math.log(1000.0)
    strong = jnp.exp(jax.random.uniform(second, (NZ, ROWS, NX), jnp.float32, strong_low, strong_high))
    picked = jax.random.randint(third, (1, ROWS, NX), 0, 4) == 0
    return jnp.where(picked, strong, base).astype(jnp.float32)


def draw_ocean_levels(key, part):
    first, second = jax.random.split(jax.random.fold_in(key, 83), 2)
    full_depth = jax.random.randint(first, (ROWS, NX), 0, 2) == 0
    partial_value = jax.random.randint(second, (ROWS, NX), 0, NZ + 1)
    return jnp.where(full_depth, NZ, partial_value).astype(jnp.int32)


def level_of(stream_key, shape, cuts, least, high):
    gain = 1.0
    for axis_at, parts in cuts:
        heights = jax.random.uniform(jax.random.fold_in(jax.random.fold_in(stream_key, 6), axis_at), (parts,), jnp.float32, least / len(cuts), high / len(cuts))
        gain = gain * jnp.repeat(jnp.exp(heights), shape[axis_at] // parts).reshape((-1,) + (1,) * (len(shape) - 1 - axis_at))
    return gain


def normal_values(rng, dims, width, most, pieces=(), held_as=jnp.bfloat16):
    level = level_of(rng, dims, pieces, -0.22, 0.18) if pieces else 1.0
    array = jax.random.normal(rng, dims, jnp.float32) * width * level
    return jnp.minimum(jnp.maximum(array, -most), most).astype(held_as)


def setup_inputs(seed: int = 0) -> dict:
    key_of = jax.random.split(jax.random.key(seed), 9)
    return {
        "tracer_adjoint": normal_values(key_of[0], (2, NZ, ROWS, NX), 1.0, 6.0, ((1, 32), (2, 16)), jnp.float32),
        "surface_adjoint": normal_values(key_of[1], (ROWS, NX), 1.0, 6.0, ((0, 16), (1, 32)), jnp.float32),
        "velocity": jnp.clip(jax.random.uniform(key_of[2], (2, NZ, ROWS, NX), jnp.float32, -0.5, 0.5) * level_of(key_of[2], (2, NZ, ROWS, NX), ((1, 32), (2, 16)), -0.4, 0.0), -0.5, 0.5).astype(jnp.bfloat16),
        "vertical_coupling": draw_vertical_coupling(jax.random.fold_in(key_of[8], 71), 0),
        "ocean_levels": draw_ocean_levels(jax.random.fold_in(key_of[8], 71), 0),
        "face_conductance": draw_face_conductance(jax.random.fold_in(key_of[8], 71), 0),
        "buoyancy_weights": jnp.clip(jax.random.uniform(key_of[6], (2, NZ), jnp.float32, -1.0, 1.0), -1.0, 1.0),
        "surface_flux": jnp.clip(jax.random.uniform(key_of[7], (2,), jnp.float32, 0.5, 2.0), 0.5, 2.0),
    }


DIFFUSION = 0.1


def wet_mask(ocean_levels, levels):
    depth_index = lax.broadcasted_iota(jnp.int32, (levels,) + ocean_levels.shape, 0)
    return (depth_index < ocean_levels[None]).astype(jnp.float32)


def thomas_factor(coupling, wet_cells):
    upper_wet = jnp.concatenate([jnp.zeros_like(wet_cells[:1]), wet_cells[:-1]], axis=0)
    couplings = coupling * wet_cells * upper_wet
    lower_links = jnp.concatenate([couplings[1:], jnp.zeros_like(couplings[:1])], axis=0)
    diagonal = 1.0 + couplings + lower_links

    def factor_level(previous, layer):
        level_diag, level_coup, level_low = layer
        reciprocal = 1.0 / (level_diag - level_coup * previous)
        following = level_low * reciprocal
        return following, (reciprocal, following)

    _, (inverse, forward) = lax.scan(factor_level, jnp.zeros_like(diagonal[0]), (diagonal, couplings, lower_links))
    return couplings, inverse, forward


def thomas_solve(source, couplings, inverse, forward):
    levels_first = jnp.swapaxes(source, 0, 1)

    def downward(previous, layer):
        level_src, level_coup, level_inv = layer
        current = (level_src + level_coup * previous) * level_inv
        return current, current

    _, partial_sweep = lax.scan(downward, jnp.zeros_like(levels_first[0]), (levels_first, couplings, inverse))

    def upward(following, layer):
        level_part, level_fwd = layer
        current = level_part + level_fwd * following
        return current, current

    _, solution = lax.scan(upward, jnp.zeros_like(levels_first[0]), (partial_sweep, forward), reverse=True)
    return jnp.swapaxes(solution, 0, 1)


def relax_surface(source, conductance, reciprocal, extend):
    def sweep(sweep_index, iterate):
        padded = extend(iterate)
        summed = (source + conductance[0] * padded[1:-1, 2:] + conductance[1] * padded[1:-1, :-2]
                  + conductance[2] * padded[2:, 1:-1] + conductance[3] * padded[:-2, 1:-1])
        return summed * reciprocal
    return lax.fori_loop(0, SOLVE_ITERS, sweep, source)


def horizontal(center, gradient, east_flux, north_flux):
    laplace = (gradient[..., 1:-1, 2:] + gradient[..., 1:-1, :-2] + gradient[..., 2:, 1:-1]
               + gradient[..., :-2, 1:-1] - 4.0 * center)
    return (center + DIFFUSION * laplace + 0.5 * (east_flux[..., 1:-1, 2:] - east_flux[..., 1:-1, :-2])
            + 0.5 * (north_flux[..., 2:, 1:-1] - north_flux[..., :-2, 1:-1]))


def pad_surface(iterate):
    return jnp.pad(iterate, 1)


def pad_cells(values):
    return jnp.pad(values, ((0, 0), (0, 0), (1, 1), (1, 1)))


def reference(tracer_adjoint, surface_adjoint, velocity, vertical_coupling, ocean_levels, face_conductance, buoyancy_weights, surface_flux):
    wet_cells = wet_mask(ocean_levels, NZ)
    couplings, inverse, forward = thomas_factor(vertical_coupling, wet_cells)
    reciprocal = 1.0 / (1.0 + face_conductance[0] + face_conductance[1] + face_conductance[2] + face_conductance[3])
    weighted = buoyancy_weights[:, :, None, None] * wet_cells[None]
    zonal = velocity[0].astype(jnp.float32)
    meridional = velocity[1].astype(jnp.float32)
    tracer_grad = tracer_adjoint
    surface_grad = surface_adjoint
    for step_index in range(STEPS):
        relaxed = relax_surface(surface_grad, face_conductance, reciprocal, pad_surface)
        column_grad = tracer_grad + weighted * relaxed[None, None]
        mixed_grad = thomas_solve(column_grad, couplings, inverse, forward)
        surface_grad = relaxed + wet_cells[0] * jnp.sum(surface_flux[:, None, None] * mixed_grad[:, 0], axis=0)
        masked_grad = wet_cells[None] * mixed_grad
        tracer_grad = horizontal(masked_grad, pad_cells(masked_grad), pad_cells(zonal * masked_grad),
                                 pad_cells(meridional * masked_grad))
    return tracer_grad, surface_grad
```

```python
import functools

import jax
import jax.numpy as jnp
from jax import lax
from jax.experimental import pallas as pl
from jax.experimental.pallas import tpu as pltpu
from jax.sharding import PartitionSpec as P

SOLVE_ITERS = 12
STEPS = 2
DIFFUSION = 0.1
MESH = pl.DeviceIdType.MESH
ROWS = 8
LANES = 128
UP, SIDE = 2, 1
HIGH, WIDE = (2 * UP + 1) * ROWS, (2 * SIDE + 1) * LANES


def wrap(value, size):
    return lax.rem(value + 2 * size, size)


def push(src, dst, send_sem, recv_sem, device):
    copy = pltpu.make_async_remote_copy(
        src_ref=src,
        dst_ref=dst,
        send_sem=send_sem,
        recv_sem=recv_sem,
        device_id=device,
        device_id_type=MESH,
    )
    return copy


def landed(ref, sem):
    pltpu.make_async_copy(ref, ref, sem).wait()


def kernel(
    sizes,
    tracer,
    surface,
    velocity,
    coupling,
    ocean_levels,
    conductance,
    weights,
    flux,
    tracer_out,
    surface_out,
    columns,
    currents,
    back,
    cond_region,
    surf_region,
    folded,
    inverse,
    lower,
    forward,
    grad,
    partial,
    surf_block,
    lane_send,
    lane_recv,
    row_send,
    row_recv,
    column_sems,
    current_sems,
    back_sems,
    cond_sems,
    surf_sems,
    lane_sems,
    row_sems,
):
    groups, tiles, share, levels = sizes
    group = lax.axis_index("grp")
    tile = lax.axis_index("tile")
    depth = ocean_levels[...]

    near = [
        (a, b)
        for a in range(2 * UP + 1)
        for b in range(2 * SIDE + 1)
        if (a, b) != (UP, SIDE)
    ]

    def near_device(a, b):
        return (wrap(group - (a - UP), groups), wrap(tile - (b - SIDE), tiles))

    barrier = pltpu.get_barrier_semaphore()

    def greet(i, _):
        pl.semaphore_signal(
            barrier, inc=1, device_id=(group, wrap(tile + i, tiles)), device_id_type=MESH
        )
        return 0

    lax.fori_loop(1, tiles, greet, 0)
    greeted = tiles - 1
    for a, b in near:
        if a != UP:
            greeted += 1
            pl.semaphore_signal(barrier, inc=1, device_id=near_device(a, b), device_id_type=MESH)
    pl.semaphore_wait(barrier, greeted)

    def block(a, b):
        return (pl.ds(a * ROWS, ROWS), pl.ds(b * LANES, LANES))

    def cond_copy(n):
        a, b = near[n]
        rows, lanes = block(a, b)
        return push(
            conductance,
            cond_region.at[:, rows, lanes],
            cond_sems.at[0, n],
            cond_sems.at[1, n],
            near_device(a, b),
        )

    def surf_copy(step, n):
        a, b = near[n]
        rows, lanes = block(a, b)
        return push(
            surface if step == 0 else surf_block,
            surf_region.at[step, rows, lanes],
            surf_sems.at[step, 0, n],
            surf_sems.at[step, 1, n],
            near_device(a, b),
        )

    for n in range(len(near)):
        cond_copy(n).start()
        surf_copy(0, n).start()

    def lanes_of(i):
        return pl.ds(pl.multiple_of(i * LANES, LANES), LANES)

    def column_copy(to):
        return push(
            tracer.at[:, :, :, lanes_of(to)],
            columns.at[:, pl.ds(tile * share, share)],
            column_sems.at[0, to],
            column_sems.at[1, tile],
            (group, to),
        )

    def current_copy(to):
        return push(
            velocity.at[:, :, :, lanes_of(to)],
            currents.at[:, pl.ds(tile * share, share)],
            current_sems.at[0, to],
            current_sems.at[1, tile],
            (group, to),
        )

    def back_copy(to):
        return push(
            partial.at[:, pl.ds(to * share, share)],
            back.at[:, :, :, lanes_of(tile)],
            back_sems.at[0, to],
            back_sems.at[1, tile],
            (group, to),
        )

    def others(action):
        def one(i, _):
            action(wrap(tile + i, tiles))
            return 0

        lax.fori_loop(1, tiles, one, 0)

    others(lambda to: column_copy(to).start())
    own_column = pltpu.make_async_copy(
        tracer.at[:, :, :, lanes_of(tile)],
        columns.at[:, pl.ds(tile * share, share)],
        column_sems.at[1, tile],
    )
    own_column.start()
    others(lambda to: current_copy(to).start())
    own_current = pltpu.make_async_copy(
        velocity.at[:, :, :, lanes_of(tile)],
        currents.at[:, pl.ds(tile * share, share)],
        current_sems.at[1, tile],
    )
    own_current.start()

    own_rows, own_lanes = block(UP, SIDE)
    cond_region[:, own_rows, own_lanes] = conductance[...]
    surf_region[0, own_rows, own_lanes] = surface[...]

    def factor(k, carry):
        previous, level_coup = carry
        following = jnp.where(k + 1 < depth, coupling[jnp.minimum(k + 1, levels - 1)], 0.0)
        diagonal = 1.0 + level_coup + following
        reciprocal = 1.0 / (diagonal - level_coup * previous)
        ahead = following * reciprocal
        inverse[k] = reciprocal
        lower[k] = level_coup * reciprocal
        forward[k] = ahead
        return (ahead, following)

    nothing = jnp.zeros((ROWS, LANES), jnp.float32)
    lax.fori_loop(0, levels, factor, (nothing, nothing))

    row_at = lax.broadcasted_iota(jnp.int32, (HIGH, WIDE), 0) + (group - UP) * ROWS
    lane_at = lax.broadcasted_iota(jnp.int32, (HIGH, WIDE), 1) + (tile - SIDE) * LANES
    inside = (
        (row_at >= 0)
        & (row_at < groups * ROWS)
        & (lane_at >= 0)
        & (lane_at < tiles * LANES)
    )

    for n in range(len(near)):
        rows, lanes = block(*near[n])
        landed(cond_region.at[:, rows, lanes], cond_sems.at[1, n])
    faces = [jnp.where(inside, cond_region[f], 0.0) for f in range(4)]
    region_recip = 1.0 / (1.0 + faces[0] + faces[1] + faces[2] + faces[3])
    for f in range(4):
        folded[f] = faces[f] * region_recip
    folded[4] = region_recip

    def relax(step):
        for n in range(len(near)):
            rows, lanes = block(*near[n])
            landed(surf_region.at[step, rows, lanes], surf_sems.at[step, 1, n])
        source = jnp.where(inside, surf_region[step], 0.0)
        scaled = source * folded[4]

        def sweep(_, iterate):
            return (
                scaled
                + folded[0] * pltpu.roll(iterate, WIDE - 1, 1)
                + folded[1] * pltpu.roll(iterate, 1, 1)
                + folded[2] * pltpu.roll(iterate, HIGH - 1, 0)
                + folded[3] * pltpu.roll(iterate, 1, 0)
            )

        solved = lax.fori_loop(0, SOLVE_ITERS, sweep, source)
        return solved[UP * ROWS : (UP + 1) * ROWS, SIDE * LANES : (SIDE + 1) * LANES]

    lane = lax.broadcasted_iota(jnp.int32, (ROWS, LANES), 1)
    row = lax.broadcasted_iota(jnp.int32, (ROWS, LANES), 0)

    def downward(k, sources, relaxed, carry):
        wet = jnp.where(k < depth, relaxed, 0.0)
        level_inv, level_low = inverse[k], lower[k]
        done = []
        for a in range(2):
            current = (sources[a] + weights[a, k] * wet) * level_inv + level_low * carry[a]
            grad[a, k] = current
            done.append(current)
        return tuple(done)

    def upward():
        def one(j, carry):
            for u in range(share):
                k = levels - 1 - (j * share + u)
                ahead = forward[k]
                wet = k < depth
                carry = tuple(grad[a, k] + ahead * carry[a] for a in range(2))
                for a in range(2):
                    grad[a, k] = jnp.where(wet, carry[a], 0.0)
            return carry

        return lax.fori_loop(0, tiles, one, (nothing, nothing))

    def next_surface(relaxed, top):
        return relaxed + jnp.where(0 < depth, flux[0] * top[0] + flux[1] * top[1], 0.0)

    def spread(step):
        def one(j, carry):
            carry = list(carry)
            for u in range(share):
                k = j * share + u
                zonal = 0.5 * currents[0, k].astype(jnp.float32)
                meridional = 0.5 * currents[1, k].astype(jnp.float32)
                to_west, to_east = DIFFUSION + zonal, DIFFUSION - zonal
                to_south, to_north = DIFFUSION + meridional, DIFFUSION - meridional
                for a in range(2):
                    masked = grad[a, k]
                    from_east = pltpu.roll(masked * to_west, LANES - 1, 1)
                    from_west = pltpu.roll(masked * to_east, 1, 1)
                    southward = masked * to_south
                    from_north = pltpu.roll(southward, ROWS - 1, 0)
                    from_south = pltpu.roll(masked * to_north, 1, 0)
                    partial[a, k] = (
                        (1.0 - 4.0 * DIFFUSION) * masked
                        + jnp.where(lane == LANES - 1, 0.0, from_east)
                        + jnp.where(lane == 0, 0.0, from_west)
                        + jnp.where(row == ROWS - 1, 0.0, from_north)
                        + jnp.where(row == 0, 0.0, from_south)
                    )
                    carry[2 * a] = jnp.where(
                        lane == k, pltpu.roll(from_east, k + 1, 1), carry[2 * a]
                    )
                    carry[2 * a + 1] = jnp.where(
                        lane == k, pltpu.roll(from_west, k, 1), carry[2 * a + 1]
                    )
                    row_send[step, 0, a, pl.ds(k, 1), :] = southward[0:1]
                    row_send[step, 1, a, pl.ds(k, 1), :] = from_south[0:1]
            return tuple(carry)

        edges = lax.fori_loop(0, tiles, one, (nothing,) * 4)
        for a in range(2):
            for side in range(2):
                lane_send[step, side, a] = edges[2 * a + side]

    def edge_copies(step):
        return [
            push(
                lane_send.at[step, side],
                lane_recv.at[step, side],
                lane_sems.at[step, 0, side],
                lane_sems.at[step, 1, side],
                (group, wrap(tile - 1 + 2 * side, tiles)),
            )
            for side in range(2)
        ] + [
            push(
                row_send.at[step, side],
                row_recv.at[step, side],
                row_sems.at[step, 0, side],
                row_sems.at[step, 1, side],
                (wrap(group - 1 + 2 * side, groups), tile),
            )
            for side in range(2)
        ]

    def edges_landed(step):
        for side in range(2):
            landed(lane_recv.at[step, side], lane_sems.at[step, 1, side])
            landed(row_recv.at[step, side], row_sems.at[step, 1, side])

    at_east = (lane == LANES - 1) & (tile < tiles - 1)
    at_west = (lane == 0) & (tile > 0)
    at_north = (row == ROWS - 1) & (group < groups - 1)
    at_south = (row == 0) & (group > 0)

    def gathered(step, a, k):
        east = pltpu.roll(lane_recv[step, 0, a], LANES - 1 - k, 1)
        west = pltpu.roll(lane_recv[step, 1, a], LANES - k, 1)
        north = jnp.broadcast_to(row_recv[step, 0, a, pl.ds(k, 1), :], (ROWS, LANES))
        south = jnp.broadcast_to(row_recv[step, 1, a, pl.ds(k, 1), :], (ROWS, LANES))
        return (
            partial[a, k]
            + jnp.where(at_east, east, 0.0)
            + jnp.where(at_west, west, 0.0)
            + jnp.where(at_north, north, 0.0)
            + jnp.where(at_south, south, 0.0)
        )

    relaxed = relax(0)

    def first_down(s, carry):
        landed(columns.at[:, pl.ds(s * share, share)], column_sems.at[1, s])
        for u in range(share):
            k = s * share + u
            carry = downward(k, [columns[0, k], columns[1, k]], relaxed, carry)
        return carry

    lax.fori_loop(0, tiles, first_down, (nothing, nothing))
    top = upward()
    surf_block[...] = next_surface(relaxed, top)
    surf_region[1, own_rows, own_lanes] = surf_block[...]
    for n in range(len(near)):
        surf_copy(1, n).start()

    def current_landed(s, _):
        landed(currents.at[:, pl.ds(s * share, share)], current_sems.at[1, s])
        return 0

    lax.fori_loop(0, tiles, current_landed, 0)
    spread(0)
    for copy in edge_copies(0):
        copy.start()

    relaxed_again = relax(1)
    edges_landed(0)

    def second_down(s, carry):
        for u in range(share):
            k = s * share + u
            carry = downward(k, [gathered(0, a, k) for a in range(2)], relaxed_again, carry)
        return carry

    lax.fori_loop(0, tiles, second_down, (nothing, nothing))
    top = upward()
    surface_out[...] = next_surface(relaxed_again, top)
    spread(1)
    for copy in edge_copies(1):
        copy.start()
    edges_landed(1)

    def finish(i, _):
        to = wrap(tile + i, tiles)
        for u in range(share):
            k = to * share + u
            for a in range(2):
                partial[a, k] = gathered(1, a, k)
        return 0

    lax.fori_loop(0, tiles, finish, 0)
    others(lambda to: back_copy(to).start())
    own_back = pltpu.make_async_copy(
        partial.at[:, pl.ds(tile * share, share)],
        back.at[:, :, :, lanes_of(tile)],
        back_sems.at[1, tile],
    )
    own_back.start()

    def back_landed(s, _):
        landed(back.at[:, :, :, lanes_of(s)], back_sems.at[1, s])
        return 0

    lax.fori_loop(0, tiles, back_landed, 0)
    tracer_out[...] = back[...]

    others(lambda to: column_copy(to).wait_send())
    others(lambda to: current_copy(to).wait_send())
    others(lambda to: back_copy(to).wait_send())
    for n in range(len(near)):
        cond_copy(n).wait_send()
        for step in range(STEPS):
            surf_copy(step, n).wait_send()
    for step in range(STEPS):
        for copy in edge_copies(step):
            copy.wait_send()


def local(
    tracer_adjoint,
    surface_adjoint,
    velocity,
    vertical_coupling,
    ocean_levels,
    face_conductance,
    buoyancy_weights,
    surface_flux,
):
    groups, tiles = lax.axis_size("grp"), lax.axis_size("tile")
    levels = vertical_coupling.shape[0]
    share = levels // tiles
    cells = (ROWS, LANES)
    near = (2 * UP + 1) * (2 * SIDE + 1) - 1
    f32 = jnp.float32
    vmem = pl.BlockSpec(memory_space=pltpu.VMEM)
    smem = pl.BlockSpec(memory_space=pltpu.SMEM)
    dma = pltpu.SemaphoreType.DMA
    return pl.pallas_call(
        functools.partial(kernel, (groups, tiles, share, levels)),
        out_shape=(
            jax.ShapeDtypeStruct(tracer_adjoint.shape, f32),
            jax.ShapeDtypeStruct(surface_adjoint.shape, f32),
        ),
        in_specs=[vmem] * 6 + [smem] * 2,
        out_specs=(vmem, vmem),
        scratch_shapes=[
            pltpu.VMEM((2, levels) + cells, f32),
            pltpu.VMEM((2, levels) + cells, jnp.bfloat16),
            pltpu.VMEM(tracer_adjoint.shape, f32),
            pltpu.VMEM((4, HIGH, WIDE), f32),
            pltpu.VMEM((STEPS, HIGH, WIDE), f32),
            pltpu.VMEM((5, HIGH, WIDE), f32),
            pltpu.VMEM((levels,) + cells, f32),
            pltpu.VMEM((levels,) + cells, f32),
            pltpu.VMEM((levels,) + cells, f32),
            pltpu.VMEM((2, levels) + cells, f32),
            pltpu.VMEM((2, levels) + cells, f32),
            pltpu.VMEM(cells, f32),
            pltpu.VMEM((STEPS, 2, 2) + cells, f32),
            pltpu.VMEM((STEPS, 2, 2) + cells, f32),
            pltpu.VMEM((STEPS, 2, 2, levels, LANES), f32),
            pltpu.VMEM((STEPS, 2, 2, levels, LANES), f32),
            dma((2, tiles)),
            dma((2, tiles)),
            dma((2, tiles)),
            dma((2, near)),
            dma((STEPS, 2, near)),
            dma((STEPS, 2, 2)),
            dma((STEPS, 2, 2)),
        ],
        compiler_params=pltpu.CompilerParams(collective_id=0, has_side_effects=True),
    )(
        tracer_adjoint,
        surface_adjoint,
        velocity,
        vertical_coupling,
        ocean_levels,
        face_conductance,
        buoyancy_weights,
        surface_flux,
    )


def solution(mesh):
    in_specs = (
        P(None, "tile", "grp", None),
        P("grp", "tile"),
        P(None, "tile", "grp", None),
        P(None, "grp", "tile"),
        P("grp", "tile"),
        P(None, "grp", "tile"),
        P(),
        P(),
    )
    out_specs = (P(None, "tile", "grp", None), P("grp", "tile"))
    return jax.shard_map(local, mesh=mesh, in_specs=in_specs, out_specs=out_specs, check_vma=False)
```

```python
import functools

import jax
import jax.numpy as jnp
from jax import lax
from jax.experimental import pallas as pl
from jax.experimental.pallas import tpu as pltpu
from jax.sharding import PartitionSpec as P

SOLVE_ITERS = 12
STEPS = 2
DIFFUSION = 0.1
CODE_MAX = 32767.0
MESH = pl.DeviceIdType.MESH
ROWS = 8
LANES = 128
UP, SIDE = 2, 1
HIGH, WIDE = (2 * UP + 1) * ROWS, (2 * SIDE + 1) * LANES


def wrap(value, size):
    return lax.rem(value + 2 * size, size)


def push(src, dst, send_sem, recv_sem, device):
    copy = pltpu.make_async_remote_copy(
        src_ref=src,
        dst_ref=dst,
        send_sem=send_sem,
        recv_sem=recv_sem,
        device_id=device,
        device_id_type=MESH,
    )
    return copy


def landed(ref, sem):
    pltpu.make_async_copy(ref, ref, sem).wait()


def block(a, b):
    return (pl.ds(a * ROWS, ROWS), pl.ds(b * LANES, LANES))


def lanes_of(i):
    return pl.ds(pl.multiple_of(i * LANES, LANES), LANES)


def decode(word):
    first = lax.shift_right_arithmetic(word + 32768, 16)
    second = word - lax.shift_left(first, 16)
    return (first.astype(jnp.float32), second.astype(jnp.float32))


def kernel(
    sizes,
    tracer_in,
    surface,
    velocity,
    coupling_in,
    ocean_levels,
    conductance,
    weights_in,
    flux_in,
    codes_out,
    scales_out,
    surface_out,
    tracer,
    coupling,
    depths,
    weights,
    flux,
    sent_codes,
    sent_scales,
    codes,
    scales,
    currents,
    back_codes,
    back_scales,
    cond_region,
    surf_region,
    folded,
    inverse,
    lower,
    forward,
    grad,
    partial,
    surf_block,
    lane_send,
    lane_recv,
    row_send,
    row_recv,
    local_sems,
    code_sems,
    scale_sems,
    current_sems,
    back_code_sems,
    back_scale_sems,
    cond_sems,
    surf_sems,
    lane_sems,
    row_sems,
):
    groups, tiles, share, levels = sizes
    group = lax.axis_index("grp")
    tile = lax.axis_index("tile")

    own_rows, own_lanes = block(UP, SIDE)
    loads = [
        pltpu.make_async_copy(src, dst, local_sems.at[n])
        for n, (src, dst) in enumerate(
            [
                (tracer_in, tracer),
                (ocean_levels, depths),
                (coupling_in, coupling),
                (weights_in, weights),
                (flux_in, flux),
                (conductance, cond_region.at[:, own_rows, own_lanes]),
                (surface, surf_region.at[0, own_rows, own_lanes]),
            ]
        )
    ]
    loads[0].start()

    near = [
        (a, b)
        for a in range(2 * UP + 1)
        for b in range(2 * SIDE + 1)
        if (a, b) != (UP, SIDE)
    ]

    def near_device(a, b):
        return (wrap(group - (a - UP), groups), wrap(tile - (b - SIDE), tiles))

    barrier = pltpu.get_barrier_semaphore()

    def greet(i, _):
        pl.semaphore_signal(
            barrier, inc=1, device_id=(group, wrap(tile + i, tiles)), device_id_type=MESH
        )
        return 0

    lax.fori_loop(1, tiles, greet, 0)
    greeted = tiles - 1
    for a, b in near:
        if a != UP:
            greeted += 1
            pl.semaphore_signal(barrier, inc=1, device_id=near_device(a, b), device_id_type=MESH)
    for load in loads[1:]:
        load.start()

    def encode(values, slot, code_ref, scale_ref):
        rounded = []
        for a in range(2):
            peak = functools.reduce(jnp.maximum, [jnp.abs(v) for v in values[a]])
            peak = jnp.maximum(jnp.max(peak, axis=0, keepdims=True), 1e-30)
            gain = jnp.broadcast_to(CODE_MAX / peak, (ROWS, LANES))
            scale_ref[slot, pl.ds(a, 1), :] = peak * (1.0 / CODE_MAX)
            rounded.append([jnp.floor(v * gain + 0.5).astype(jnp.int32) for v in values[a]])
        for u in range(share):
            code_ref[slot, u] = lax.shift_left(rounded[0][u], 16) + rounded[1][u]

    loads[0].wait()

    def encode_tracer(to, _):
        values = [[tracer[a, u, :, lanes_of(to)] for u in range(share)] for a in range(2)]
        encode(values, to, sent_codes, sent_scales)
        return 0

    lax.fori_loop(0, tiles, encode_tracer, 0)
    pl.semaphore_wait(barrier, greeted)

    def cond_copy(n):
        a, b = near[n]
        rows, lanes = block(a, b)
        return push(
            conductance,
            cond_region.at[:, rows, lanes],
            cond_sems.at[0, n],
            cond_sems.at[1, n],
            near_device(a, b),
        )

    def surf_copy(step, n):
        a, b = near[n]
        rows, lanes = block(a, b)
        return push(
            surface if step == 0 else surf_block,
            surf_region.at[step, rows, lanes],
            surf_sems.at[step, 0, n],
            surf_sems.at[step, 1, n],
            near_device(a, b),
        )

    for n in range(len(near)):
        cond_copy(n).start()
        surf_copy(0, n).start()

    def code_copies(to):
        return (
            push(
                sent_codes.at[to],
                codes.at[tile],
                code_sems.at[0, to],
                code_sems.at[1, tile],
                (group, to),
            ),
            push(
                sent_scales.at[to],
                scales.at[tile],
                scale_sems.at[0, to],
                scale_sems.at[1, tile],
                (group, to),
            ),
        )

    def current_copy(to):
        return push(
            velocity.at[:, :, :, lanes_of(to)],
            currents.at[:, pl.ds(tile * share, share)],
            current_sems.at[0, to],
            current_sems.at[1, tile],
            (group, to),
        )

    def back_copies(to):
        return (
            push(
                back_codes.at[to],
                codes_out.at[:, :, lanes_of(tile)],
                back_code_sems.at[0, to],
                back_code_sems.at[1, tile],
                (group, to),
            ),
            push(
                back_scales.at[to],
                scales_out.at[:, lanes_of(tile)],
                back_scale_sems.at[0, to],
                back_scale_sems.at[1, tile],
                (group, to),
            ),
        )

    def start(copies):
        for copy in copies:
            copy.start()

    def sent(copies):
        for copy in copies:
            copy.wait_send()

    def others(action):
        def one(i, _):
            action(wrap(tile + i, tiles))
            return 0

        lax.fori_loop(1, tiles, one, 0)

    others(lambda to: start(code_copies(to)))
    start(
        [
            pltpu.make_async_copy(sent_codes.at[tile], codes.at[tile], code_sems.at[1, tile]),
            pltpu.make_async_copy(sent_scales.at[tile], scales.at[tile], scale_sems.at[1, tile]),
        ]
    )
    others(lambda to: current_copy(to).start())
    own_current = pltpu.make_async_copy(
        velocity.at[:, :, :, lanes_of(tile)],
        currents.at[:, pl.ds(tile * share, share)],
        current_sems.at[1, tile],
    )
    own_current.start()

    for load in loads[1:]:
        load.wait()
    depth = depths[...]

    def factor(k, carry):
        previous, level_coup = carry
        following = jnp.where(k + 1 < depth, coupling[jnp.minimum(k + 1, levels - 1)], 0.0)
        diagonal = 1.0 + level_coup + following
        reciprocal = 1.0 / (diagonal - level_coup * previous)
        ahead = following * reciprocal
        inverse[k] = reciprocal
        lower[k] = level_coup * reciprocal
        forward[k] = ahead
        return (ahead, following)

    nothing = jnp.zeros((ROWS, LANES), jnp.float32)
    lax.fori_loop(0, levels, factor, (nothing, nothing))

    row_at = lax.broadcasted_iota(jnp.int32, (HIGH, WIDE), 0) + (group - UP) * ROWS
    lane_at = lax.broadcasted_iota(jnp.int32, (HIGH, WIDE), 1) + (tile - SIDE) * LANES
    inside = (
        (row_at >= 0)
        & (row_at < groups * ROWS)
        & (lane_at >= 0)
        & (lane_at < tiles * LANES)
    )

    for n in range(len(near)):
        rows, lanes = block(*near[n])
        landed(cond_region.at[:, rows, lanes], cond_sems.at[1, n])
    faces = [jnp.where(inside, cond_region[f], 0.0) for f in range(4)]
    region_recip = 1.0 / (1.0 + faces[0] + faces[1] + faces[2] + faces[3])
    for f in range(4):
        folded[f] = faces[f] * region_recip
    folded[4] = region_recip

    def relax(step):
        for n in range(len(near)):
            rows, lanes = block(*near[n])
            landed(surf_region.at[step, rows, lanes], surf_sems.at[step, 1, n])
        source = jnp.where(inside, surf_region[step], 0.0)
        scaled = source * folded[4]

        def sweep(_, iterate):
            return (
                scaled
                + folded[0] * pltpu.roll(iterate, WIDE - 1, 1)
                + folded[1] * pltpu.roll(iterate, 1, 1)
                + folded[2] * pltpu.roll(iterate, HIGH - 1, 0)
                + folded[3] * pltpu.roll(iterate, 1, 0)
            )

        solved = lax.fori_loop(0, SOLVE_ITERS, sweep, source)
        return solved[UP * ROWS : (UP + 1) * ROWS, SIDE * LANES : (SIDE + 1) * LANES]

    lane = lax.broadcasted_iota(jnp.int32, (ROWS, LANES), 1)
    row = lax.broadcasted_iota(jnp.int32, (ROWS, LANES), 0)

    def downward(k, sources, relaxed, carry):
        wet = jnp.where(k < depth, relaxed, 0.0)
        level_inv, level_low = inverse[k], lower[k]
        done = []
        for a in range(2):
            current = (sources[a] + weights[a, k] * wet) * level_inv + level_low * carry[a]
            grad[a, k] = current
            done.append(current)
        return tuple(done)

    def upward():
        def one(j, carry):
            for u in range(share):
                k = levels - 1 - (j * share + u)
                ahead = forward[k]
                wet = k < depth
                carry = tuple(grad[a, k] + ahead * carry[a] for a in range(2))
                for a in range(2):
                    grad[a, k] = jnp.where(wet, carry[a], 0.0)
            return carry

        return lax.fori_loop(0, tiles, one, (nothing, nothing))

    def next_surface(relaxed, top):
        return relaxed + jnp.where(0 < depth, flux[0] * top[0] + flux[1] * top[1], 0.0)

    def spread(step):
        def one(i, carry):
            carry = list(carry)
            j = wrap(tile - i, tiles)
            if step == 0:
                landed(currents.at[:, pl.ds(j * share, share)], current_sems.at[1, j])
            for u in range(share):
                k = j * share + u
                zonal = 0.5 * currents[0, k].astype(jnp.float32)
                meridional = 0.5 * currents[1, k].astype(jnp.float32)
                to_west, to_east = DIFFUSION + zonal, DIFFUSION - zonal
                to_south, to_north = DIFFUSION + meridional, DIFFUSION - meridional
                for a in range(2):
                    masked = grad[a, k]
                    from_east = pltpu.roll(masked * to_west, LANES - 1, 1)
                    from_west = pltpu.roll(masked * to_east, 1, 1)
                    southward = masked * to_south
                    from_north = pltpu.roll(southward, ROWS - 1, 0)
                    from_south = pltpu.roll(masked * to_north, 1, 0)
                    partial[a, k] = (
                        (1.0 - 4.0 * DIFFUSION) * masked
                        + jnp.where(lane == LANES - 1, 0.0, from_east)
                        + jnp.where(lane == 0, 0.0, from_west)
                        + jnp.where(row == ROWS - 1, 0.0, from_north)
                        + jnp.where(row == 0, 0.0, from_south)
                    )
                    carry[2 * a] = jnp.where(
                        lane == k, pltpu.roll(from_east, k + 1, 1), carry[2 * a]
                    )
                    carry[2 * a + 1] = jnp.where(
                        lane == k, pltpu.roll(from_west, k, 1), carry[2 * a + 1]
                    )
                    row_send[step, 0, a, pl.ds(k, 1), :] = southward[0:1]
                    row_send[step, 1, a, pl.ds(k, 1), :] = from_south[0:1]
            return tuple(carry)

        edges = lax.fori_loop(0, tiles, one, (nothing,) * 4)
        for a in range(2):
            for side in range(2):
                lane_send[step, side, a] = edges[2 * a + side]

    def edge_copies(step):
        return [
            push(
                lane_send.at[step, side],
                lane_recv.at[step, side],
                lane_sems.at[step, 0, side],
                lane_sems.at[step, 1, side],
                (group, wrap(tile - 1 + 2 * side, tiles)),
            )
            for side in range(2)
        ] + [
            push(
                row_send.at[step, side],
                row_recv.at[step, side],
                row_sems.at[step, 0, side],
                row_sems.at[step, 1, side],
                (wrap(group - 1 + 2 * side, groups), tile),
            )
            for side in range(2)
        ]

    def edges_landed(step):
        for side in range(2):
            landed(lane_recv.at[step, side], lane_sems.at[step, 1, side])
            landed(row_recv.at[step, side], row_sems.at[step, 1, side])

    at_east = (lane == LANES - 1) & (tile < tiles - 1)
    at_west = (lane == 0) & (tile > 0)
    at_north = (row == ROWS - 1) & (group < groups - 1)
    at_south = (row == 0) & (group > 0)

    def gathered(step, a, k):
        east = pltpu.roll(lane_recv[step, 0, a], LANES - 1 - k, 1)
        west = pltpu.roll(lane_recv[step, 1, a], LANES - k, 1)
        north = jnp.broadcast_to(row_recv[step, 0, a, pl.ds(k, 1), :], (ROWS, LANES))
        south = jnp.broadcast_to(row_recv[step, 1, a, pl.ds(k, 1), :], (ROWS, LANES))
        return (
            partial[a, k]
            + jnp.where(at_east, east, 0.0)
            + jnp.where(at_west, west, 0.0)
            + jnp.where(at_north, north, 0.0)
            + jnp.where(at_south, south, 0.0)
        )

    relaxed = relax(0)

    def first_down(s, carry):
        landed(codes.at[s], code_sems.at[1, s])
        landed(scales.at[s], scale_sems.at[1, s])
        factors = [scales[s, pl.ds(a, 1), :] for a in range(2)]
        for u in range(share):
            k = s * share + u
            values = decode(codes[s, u])
            carry = downward(k, [values[a] * factors[a] for a in range(2)], relaxed, carry)
        return carry

    lax.fori_loop(0, tiles, first_down, (nothing, nothing))
    top = upward()
    surf_block[...] = next_surface(relaxed, top)
    surf_region[1, own_rows, own_lanes] = surf_block[...]
    for n in range(len(near)):
        surf_copy(1, n).start()

    spread(0)
    for copy in edge_copies(0):
        copy.start()

    relaxed_again = relax(1)
    edges_landed(0)

    def second_down(s, carry):
        for u in range(share):
            k = s * share + u
            carry = downward(k, [gathered(0, a, k) for a in range(2)], relaxed_again, carry)
        return carry

    lax.fori_loop(0, tiles, second_down, (nothing, nothing))
    top = upward()
    surface_out[...] = next_surface(relaxed_again, top)
    spread(1)
    for copy in edge_copies(1):
        copy.start()
    edges_landed(1)

    def finish(to):
        values = [[gathered(1, a, to * share + u) for u in range(share)] for a in range(2)]
        encode(values, to, back_codes, back_scales)

    def finish_and_send(i, _):
        finish(wrap(tile + i, tiles))
        start(back_copies(wrap(tile + i - 1, tiles)))
        return 0

    finish(wrap(tile + 1, tiles))
    lax.fori_loop(2, tiles, finish_and_send, 0)
    finish(tile)
    start(back_copies(wrap(tile - 1, tiles)))
    start(
        [
            pltpu.make_async_copy(
                back_codes.at[tile], codes_out.at[:, :, lanes_of(tile)], back_code_sems.at[1, tile]
            ),
            pltpu.make_async_copy(
                back_scales.at[tile], scales_out.at[:, lanes_of(tile)], back_scale_sems.at[1, tile]
            ),
        ]
    )

    def back_landed(s, _):
        landed(codes_out.at[:, :, lanes_of(s)], back_code_sems.at[1, s])
        landed(scales_out.at[:, lanes_of(s)], back_scale_sems.at[1, s])
        return 0

    lax.fori_loop(0, tiles, back_landed, 0)

    others(lambda to: sent(code_copies(to)))
    others(lambda to: current_copy(to).wait_send())
    others(lambda to: sent(back_copies(to)))
    for n in range(len(near)):
        cond_copy(n).wait_send()
        for step in range(STEPS):
            surf_copy(step, n).wait_send()
    for step in range(STEPS):
        for copy in edge_copies(step):
            copy.wait_send()


def unpack(codes, scales, surface, tracer_out, surface_out):
    for u in range(codes.shape[0]):
        values = decode(codes[u])
        for a in range(2):
            tracer_out[a, u] = values[a] * scales[pl.ds(a, 1), :]
    surface_out[...] = surface[...]


def local(
    tracer_adjoint,
    surface_adjoint,
    velocity,
    vertical_coupling,
    ocean_levels,
    face_conductance,
    buoyancy_weights,
    surface_flux,
):
    groups, tiles = lax.axis_size("grp"), lax.axis_size("tile")
    levels = vertical_coupling.shape[0]
    share = levels // tiles
    cells = (ROWS, LANES)
    near = (2 * UP + 1) * (2 * SIDE + 1) - 1
    f32, i32 = jnp.float32, jnp.int32
    anywhere = pl.BlockSpec(memory_space=pl.ANY)
    vmem = pl.BlockSpec(memory_space=pltpu.VMEM)
    dma = pltpu.SemaphoreType.DMA
    packed = (tiles, share) + cells
    codes, scales, surface = pl.pallas_call(
        functools.partial(kernel, (groups, tiles, share, levels)),
        out_shape=(
            jax.ShapeDtypeStruct((share, ROWS, tiles * LANES), i32),
            jax.ShapeDtypeStruct((2, tiles * LANES), f32),
            jax.ShapeDtypeStruct(surface_adjoint.shape, f32),
        ),
        in_specs=[anywhere] * 8,
        out_specs=(anywhere, anywhere, vmem),
        scratch_shapes=[
            pltpu.VMEM(tracer_adjoint.shape, f32),
            pltpu.VMEM(vertical_coupling.shape, f32),
            pltpu.VMEM(cells, i32),
            pltpu.SMEM(buoyancy_weights.shape, f32),
            pltpu.SMEM(surface_flux.shape, f32),
            pltpu.VMEM(packed, i32),
            pltpu.VMEM((tiles, 2, LANES), f32),
            pltpu.VMEM(packed, i32),
            pltpu.VMEM((tiles, 2, LANES), f32),
            pltpu.VMEM((2, levels) + cells, jnp.bfloat16),
            pltpu.VMEM(packed, i32),
            pltpu.VMEM((tiles, 2, LANES), f32),
            pltpu.VMEM((4, HIGH, WIDE), f32),
            pltpu.VMEM((STEPS, HIGH, WIDE), f32),
            pltpu.VMEM((5, HIGH, WIDE), f32),
            pltpu.VMEM((levels,) + cells, f32),
            pltpu.VMEM((levels,) + cells, f32),
            pltpu.VMEM((levels,) + cells, f32),
            pltpu.VMEM((2, levels) + cells, f32),
            pltpu.VMEM((2, levels) + cells, f32),
            pltpu.VMEM(cells, f32),
            pltpu.VMEM((STEPS, 2, 2) + cells, f32),
            pltpu.VMEM((STEPS, 2, 2) + cells, f32),
            pltpu.VMEM((STEPS, 2, 2, levels, LANES), f32),
            pltpu.VMEM((STEPS, 2, 2, levels, LANES), f32),
            dma((7,)),
            dma((2, tiles)),
            dma((2, tiles)),
            dma((2, tiles)),
            dma((2, tiles)),
            dma((2, tiles)),
            dma((2, near)),
            dma((STEPS, 2, near)),
            dma((STEPS, 2, 2)),
            dma((STEPS, 2, 2)),
        ],
        compiler_params=pltpu.CompilerParams(collective_id=0, has_side_effects=True),
    )(
        tracer_adjoint,
        surface_adjoint,
        velocity,
        vertical_coupling,
        ocean_levels,
        face_conductance,
        buoyancy_weights,
        surface_flux,
    )
    return pl.pallas_call(
        unpack,
        out_shape=(
            jax.ShapeDtypeStruct(tracer_adjoint.shape, f32),
            jax.ShapeDtypeStruct(surface_adjoint.shape, f32),
        ),
        in_specs=[vmem] * 3,
        out_specs=(vmem, vmem),
    )(codes, scales, surface)


def solution(mesh):
    in_specs = (
        P(None, "tile", "grp", None),
        P("grp", "tile"),
        P(None, "tile", "grp", None),
        P(None, "grp", "tile"),
        P("grp", "tile"),
        P(None, "grp", "tile"),
        P(),
        P(),
    )
    out_specs = (P(None, "tile", "grp", None), P("grp", "tile"))
    return jax.shard_map(local, mesh=mesh, in_specs=in_specs, out_specs=out_specs, check_vma=False)
```

```python
import functools

import jax
import jax.numpy as jnp
from jax import lax
from jax.experimental import pallas as pl
from jax.experimental.pallas import tpu as pltpu
from jax.sharding import PartitionSpec as P

SOLVE_ITERS = 12
STEPS = 2
DIFFUSION = 0.1
CODE_MAX = 32767.0
MESH = pl.DeviceIdType.MESH
ROWS = 8
LANES = 128
UP = 2
HIGH = (2 * UP + 1) * ROWS
EDGE = 16
FIELDS = 4
QUAD = 4
CHUNKS = 2
EARLY = 8


def wrap(value, size):
    return lax.rem(value + 2 * size, size)


def push(src, dst, send_sem, recv_sem, device):
    return pltpu.make_async_remote_copy(
        src_ref=src,
        dst_ref=dst,
        send_sem=send_sem,
        recv_sem=recv_sem,
        device_id=device,
        device_id_type=MESH,
    )


def landed(ref, sem):
    pltpu.make_async_copy(ref, ref, sem).wait()


def lanes_of(i):
    return pl.ds(pl.multiple_of(i * LANES, LANES), LANES)


def decode(word):
    first = lax.shift_right_arithmetic(word + 32768, 16)
    second = word - lax.shift_left(first, 16)
    return (first.astype(jnp.float32), second.astype(jnp.float32))


def kernel(
    sizes,
    tracer_in,
    surface_in,
    velocity,
    coupling_in,
    ocean_levels,
    conductance_in,
    weights_in,
    flux_in,
    codes_out,
    scales_out,
    surface_out,
    tracer,
    surface,
    coupling,
    depths,
    conductance,
    weights,
    flux,
    sent_codes,
    sent_scales,
    codes,
    scales,
    currents,
    back_codes,
    back_scales,
    mine,
    mine_edge,
    middle,
    sides,
    around,
    fields,
    folded,
    inverse,
    lower,
    forward,
    grad,
    partial,
    surf_block,
    lane_send,
    lane_recv,
    row_send,
    row_recv,
    load_sems,
    code_sems,
    scale_sems,
    current_sems,
    send_sems,
    back_sems,
    near_sems,
    lane_sems,
    row_sems,
):
    groups, tiles, share, levels = sizes
    quads = tiles // QUAD
    deep = QUAD * share
    group = lax.axis_index("grp")
    tile = lax.axis_index("tile")
    near = [
        (a, b) for a in range(2 * UP + 1) for b in range(3) if (a, b) != (UP, 1)
    ]

    def near_device(a, b):
        return (wrap(group - (a - UP), groups), wrap(tile - (b - 1), tiles))

    loads = [
        pltpu.make_async_copy(src, dst, load_sems.at[n])
        for n, (src, dst) in enumerate(
            [
                (tracer_in, tracer),
                (conductance_in, conductance),
                (surface_in, surface),
                (ocean_levels, depths),
                (coupling_in, coupling),
                (weights_in, weights),
                (flux_in, flux),
            ]
        )
    ]
    loads[0].start()

    barrier = pltpu.get_barrier_semaphore()

    def greet(i, _):
        pl.semaphore_signal(
            barrier, inc=1, device_id=(group, wrap(tile + i, tiles)), device_id_type=MESH
        )
        return 0

    lax.fori_loop(1, tiles, greet, 0)
    greeted = tiles - 1
    for a, b in near:
        if a != UP:
            greeted += 1
            pl.semaphore_signal(barrier, inc=1, device_id=near_device(a, b), device_id_type=MESH)
    for load in loads[1:]:
        load.start()
    pl.semaphore_wait(barrier, greeted)

    def others(action, first=1, last=tiles):
        def one(i, _):
            action(wrap(tile + i, tiles))
            return 0

        lax.fori_loop(first, last, one, 0)

    def send_current(to):
        push(
            velocity.at[:, :, :, lanes_of(to)],
            currents.at[:, pl.ds(tile * share, share)],
            send_sems.at[0],
            current_sems.at[tile],
            (group, to),
        ).start()

    others(send_current, 1, 1 + EARLY)
    pltpu.make_async_copy(
        velocity.at[:, :, :, lanes_of(tile)],
        currents.at[:, pl.ds(tile * share, share)],
        current_sems.at[tile],
    ).start()

    lane = lax.broadcasted_iota(jnp.int32, (ROWS, LANES), 1)
    row = lax.broadcasted_iota(jnp.int32, (ROWS, LANES), 0)
    loads[1].wait()
    loads[2].wait()
    own = [
        conductance[0],
        conductance[2],
        1.0 / (1.0 + conductance[0] + conductance[1] + conductance[2] + conductance[3]),
        surface[...],
    ]
    packed = own[0]
    for f in range(FIELDS):
        mine[f] = own[f]
        western = own[f] if f == 0 else pltpu.roll(own[f], EDGE * f, 1)
        eastern = pltpu.roll(own[f], LANES // 2 + EDGE * (f + 1), 1)
        packed = jnp.where((lane >= EDGE * f) & (lane < EDGE * (f + 1)), western, packed)
        packed = jnp.where(
            (lane >= LANES // 2 + EDGE * f) & (lane < LANES // 2 + EDGE * (f + 1)), eastern, packed
        )
    mine_edge[...] = packed

    def encode(values, slot, code_ref, scale_ref):
        rounded = []
        for a in range(2):
            peak = functools.reduce(jnp.maximum, [jnp.abs(v) for v in values[a]])
            peak = jnp.maximum(jnp.max(peak, axis=0, keepdims=True), 1e-30)
            gain = jnp.broadcast_to(CODE_MAX / peak, (ROWS, LANES))
            scale_ref[slot, pl.ds(a, 1), :] = peak * (1.0 / CODE_MAX)
            rounded.append([jnp.floor(v * gain + 0.5).astype(jnp.int32) for v in values[a]])
        for u in range(share):
            code_ref[slot, u] = lax.shift_left(rounded[0][u], 16) + rounded[1][u]

    loads[0].wait()

    def encode_tracer(to, _):
        values = [[tracer[a, u, :, lanes_of(to)] for u in range(share)] for a in range(2)]
        encode(values, to, sent_codes, sent_scales)
        return 0

    lax.fori_loop(0, tiles, encode_tracer, 0)

    def middle_slot(a):
        return a if a < UP else a - 1

    for a, b in near:
        if b == 1:
            push(
                mine,
                middle.at[middle_slot(a)],
                send_sems.at[1],
                near_sems.at[0],
                near_device(a, b),
            ).start()
        else:
            push(
                mine_edge, sides.at[a, b // 2], send_sems.at[2], near_sems.at[1], near_device(a, b)
            ).start()

    def send_codes(to):
        push(
            sent_codes.at[to], codes.at[tile], send_sems.at[3], code_sems.at[tile], (group, to)
        ).start()
        push(
            sent_scales.at[to], scales.at[tile], send_sems.at[4], scale_sems.at[tile], (group, to)
        ).start()

    others(send_codes)
    pltpu.make_async_copy(sent_codes.at[tile], codes.at[tile], code_sems.at[tile]).start()
    pltpu.make_async_copy(sent_scales.at[tile], scales.at[tile], scale_sems.at[tile]).start()
    others(send_current, 1 + EARLY, tiles)
    for load in loads[3:]:
        load.wait()
    depth = depths[...]

    def factor(k, carry):
        previous, level_coup = carry
        following = jnp.where(k + 1 < depth, coupling[jnp.minimum(k + 1, levels - 1)], 0.0)
        diagonal = 1.0 + level_coup + following
        reciprocal = 1.0 / (diagonal - level_coup * previous)
        ahead = following * reciprocal
        inverse[k] = reciprocal
        lower[k] = level_coup * reciprocal
        forward[k] = ahead
        return (ahead, following)

    nothing = jnp.zeros((ROWS, LANES), jnp.float32)
    lax.fori_loop(0, levels, factor, (nothing, nothing))

    row_inside = [
        (group + (a - UP) >= 0) & (group + (a - UP) < groups) for a in range(2 * UP + 1)
    ]
    east_lanes = lane < EDGE
    side_inside = (east_lanes & (tile < tiles - 1)) | ((lane >= LANES - EDGE) & (tile > 0))

    def place(f, a, middle_block, side_block):
        rows = pl.ds(a * ROWS, ROWS)
        fields[f, rows, pl.ds(0, LANES)] = jnp.where(row_inside[a], middle_block, 0.0)
        fields[f, rows, pl.ds(LANES, LANES)] = jnp.where(
            side_inside & row_inside[a], side_block, 0.0
        )

    landed(middle, near_sems.at[0])
    landed(sides, near_sems.at[1])
    for a in range(2 * UP + 1):
        from_west, from_east = sides[a, 0], sides[a, 1]
        for f in range(FIELDS):
            east = from_east if f == 0 else pltpu.roll(from_east, LANES - EDGE * f, 1)
            west = pltpu.roll(from_west, (LANES // 2 - EDGE * (f + 1)) % LANES, 1)
            place(
                f,
                a,
                mine[f] if a == UP else middle[middle_slot(a), f],
                jnp.where(east_lanes, east, west),
            )
    eastern, northern, region_recip = fields[0], fields[1], fields[2]
    folded[0] = eastern * region_recip
    folded[1] = pltpu.roll(eastern, 1, 1) * region_recip
    folded[2] = northern * region_recip
    folded[3] = pltpu.roll(northern, 1, 0) * region_recip

    def relax():
        source = fields[FIELDS - 1]
        scaled = source * fields[2]

        def sweep(_, iterate):
            return (
                scaled
                + folded[0] * pltpu.roll(iterate, 2 * LANES - 1, 1)
                + folded[1] * pltpu.roll(iterate, 1, 1)
                + folded[2] * pltpu.roll(iterate, HIGH - 1, 0)
                + folded[3] * pltpu.roll(iterate, 1, 0)
            )

        solved = lax.fori_loop(0, SOLVE_ITERS, sweep, source)
        return solved[UP * ROWS : (UP + 1) * ROWS, :LANES]

    def downward(k, sources, relaxed, carry):
        wet = jnp.where(k < depth, relaxed, 0.0)
        level_inv, level_low = inverse[k], lower[k]
        done = []
        for a in range(2):
            current = (sources[a] + weights[a, k] * wet) * level_inv + level_low * carry[a]
            grad[a, k] = current
            done.append(current)
        return tuple(done)

    def upward():
        def rise(j, carry):
            for u in range(deep):
                k = levels - 1 - (j * deep + u)
                ahead = forward[k]
                wet = k < depth
                carry = tuple(grad[a, k] + ahead * carry[a] for a in range(2))
                for a in range(2):
                    grad[a, k] = jnp.where(wet, carry[a], 0.0)
            return carry

        return lax.fori_loop(0, quads, rise, (nothing, nothing))

    def next_surface(relaxed, top):
        return relaxed + jnp.where(0 < depth, flux[0] * top[0] + flux[1] * top[1], 0.0)

    def row_place(quad, u):
        return (lax.rem(quad, CHUNKS), lax.div(quad, CHUNKS) * deep + u)

    def give(step, quad, carry):
        carry = list(carry)
        for u in range(deep):
            k = quad * deep + u
            chunk, place_at = row_place(quad, u)
            zonal = 0.5 * currents[0, k].astype(jnp.float32)
            meridional = 0.5 * currents[1, k].astype(jnp.float32)
            for a in range(2):
                masked = grad[a, k]
                westward = masked * (DIFFUSION + zonal)
                eastward = masked * (DIFFUSION - zonal)
                southward = masked * (DIFFUSION + meridional)
                northward = pltpu.roll(masked * (DIFFUSION - meridional), 1, 0)
                partial[a, k] = (
                    (1.0 - 4.0 * DIFFUSION) * masked
                    + jnp.where(lane == LANES - 1, 0.0, pltpu.roll(westward, LANES - 1, 1))
                    + jnp.where(lane == 0, 0.0, pltpu.roll(eastward, 1, 1))
                    + jnp.where(row == ROWS - 1, 0.0, pltpu.roll(southward, ROWS - 1, 0))
                    + jnp.where(row == 0, 0.0, northward)
                )
                at_level = lane == k
                carry[2 * a] = jnp.where(at_level, pltpu.roll(westward, k, 1), carry[2 * a])
                carry[2 * a + 1] = jnp.where(
                    at_level, pltpu.roll(eastward, k + 1, 1), carry[2 * a + 1]
                )
                row_send[step, 0, chunk, a, pl.ds(place_at, 1), :] = southward[0:1]
                row_send[step, 1, chunk, a, pl.ds(place_at, 1), :] = northward[0:1]
        return tuple(carry)

    def keep_edges(message, edges):
        for a in range(2):
            for side in range(2):
                lane_send[message, side, a] = edges[2 * a + side]

    def edge_copies(step, chunk=None):
        message = 0 if chunk is None else 1 + chunk
        copies = []
        for side in range(2):
            rows = [ref.at[step, side] for ref in (row_send, row_recv)]
            if chunk is not None:
                rows = [ref.at[chunk] for ref in rows]
            copies += [
                push(
                    lane_send.at[message, side],
                    lane_recv.at[message, side],
                    lane_sems.at[message, 0, side],
                    lane_sems.at[message, 1, side],
                    (group, wrap(tile - 1 + 2 * side, tiles)),
                ),
                push(
                    rows[0],
                    rows[1],
                    row_sems.at[message, 0, side],
                    row_sems.at[message, 1, side],
                    (wrap(group - 1 + 2 * side, groups), tile),
                ),
            ]
        return copies

    at_east = (lane == LANES - 1) & (tile < tiles - 1)
    at_west = (lane == 0) & (tile > 0)
    at_north = (row == ROWS - 1) & (group < groups - 1)
    at_south = (row == 0) & (group > 0)

    def gathered(step, message, a, quad, u):
        k = quad * deep + u
        chunk, place_at = row_place(quad, u)
        east = pltpu.roll(lane_recv[message, 0, a], LANES - 1 - k, 1)
        west = pltpu.roll(lane_recv[message, 1, a], LANES - k, 1)
        north = row_recv[step, 0, chunk, a, pl.ds(place_at, 1), :]
        south = row_recv[step, 1, chunk, a, pl.ds(place_at, 1), :]
        return (
            partial[a, k]
            + jnp.where(at_east, east, 0.0)
            + jnp.where(at_west, west, 0.0)
            + jnp.where(at_north, jnp.broadcast_to(north, (ROWS, LANES)), 0.0)
            + jnp.where(at_south, jnp.broadcast_to(south, (ROWS, LANES)), 0.0)
        )

    relaxed = relax()

    def first_down(s, carry):
        landed(codes.at[s], code_sems.at[s])
        landed(scales.at[s], scale_sems.at[s])
        factors = [scales[s, pl.ds(a, 1), :] for a in range(2)]
        for u in range(share):
            k = s * share + u
            values = decode(codes[s, u])
            carry = downward(k, [values[a] * factors[a] for a in range(2)], relaxed, carry)
        return carry

    lax.fori_loop(0, tiles, first_down, (nothing, nothing))
    top = upward()
    surf_block[...] = next_surface(relaxed, top)

    def arrived_give(i, carry):
        quad = wrap(lax.div(tile, QUAD) - i, quads)
        for v in range(QUAD):
            s = quad * QUAD + v
            landed(currents.at[:, pl.ds(s * share, share)], current_sems.at[s])
        return give(0, quad, carry)

    edges = arrived_give(0, (nothing,) * 4)
    for n, (a, b) in enumerate(near):
        push(
            surf_block, around.at[n], send_sems.at[5], near_sems.at[2], near_device(a, b)
        ).start()
    edges = lax.fori_loop(1, quads, arrived_give, edges)
    keep_edges(0, edges)

    landed(around.at[pl.ds(0, len(near))], near_sems.at[2])
    for copy in edge_copies(0):
        copy.start()
    for a in range(2 * UP + 1):
        blocks = [surf_block if (a, b) == (UP, 1) else around.at[near.index((a, b))] for b in range(3)]
        place(FIELDS - 1, a, blocks[1][...], jnp.where(east_lanes, blocks[2][...], blocks[0][...]))
    relaxed_again = relax()
    for copy in edge_copies(0):
        copy.wait_recv()

    def second_down(quad, carry):
        for u in range(deep):
            sources = [gathered(0, 0, a, quad, u) for a in range(2)]
            carry = downward(quad * deep + u, sources, relaxed_again, carry)
        return carry

    lax.fori_loop(0, quads, second_down, (nothing, nothing))
    top = upward()
    surface_out[...] = next_surface(relaxed_again, top)

    turn = lax.div(lax.div(tile, QUAD), CHUNKS)

    def quad_of(chunk, i):
        return wrap(turn - i, quads // CHUNKS) * CHUNKS + chunk

    for chunk in range(CHUNKS):
        edges = lax.fori_loop(
            0,
            quads // CHUNKS,
            lambda i, carry, chunk=chunk: give(1, quad_of(chunk, i), carry),
            (nothing,) * 4,
        )
        keep_edges(1 + chunk, edges)
        for copy in edge_copies(1, chunk):
            copy.start()

    landed(currents.at[:, pl.ds(0, levels - share)], send_sems.at[0])
    landed(middle, send_sems.at[1])
    landed(sides, send_sems.at[2])
    landed(sent_codes.at[pl.ds(0, tiles - 1)], send_sems.at[3])
    landed(sent_scales.at[pl.ds(0, tiles - 1)], send_sems.at[4])
    landed(around.at[pl.ds(0, len(near))], send_sems.at[5])
    for copy in edge_copies(0):
        copy.wait_send()

    def back_refs(to):
        return [
            (back_codes.at[to], codes_out.at[:, :, lanes_of(tile)], 0),
            (back_scales.at[to], scales_out.at[:, lanes_of(tile)], 1),
        ]

    def send_back(quad):
        for v in range(QUAD):
            to = quad * QUAD + v

            @pl.when(to != tile)
            def _():
                for src, dst, n in back_refs(to):
                    push(src, dst, send_sems.at[6 + n], back_sems.at[n], (group, to)).start()

    for chunk in range(CHUNKS):
        for copy in edge_copies(1, chunk):
            copy.wait_recv()

        def finish(i, _, chunk=chunk):
            quad = quad_of(chunk, i)
            for v in range(QUAD):
                values = [
                    [gathered(1, 1 + chunk, a, quad, v * share + u) for u in range(share)]
                    for a in range(2)
                ]
                encode(values, quad * QUAD + v, back_codes, back_scales)

            @pl.when(i > 0)
            def _():
                send_back(quad_of(chunk, i - 1))

            return 0

        lax.fori_loop(0, quads // CHUNKS, finish, 0)
        send_back(quad_of(chunk, quads // CHUNKS - 1))
    for src, dst, n in back_refs(tile):
        pltpu.make_async_copy(src, dst, back_sems.at[n]).start()

    for chunk in range(CHUNKS):
        for copy in edge_copies(1, chunk):
            copy.wait_send()
    landed(back_codes.at[pl.ds(0, tiles - 1)], send_sems.at[6])
    landed(back_scales.at[pl.ds(0, tiles - 1)], send_sems.at[7])
    landed(codes_out, back_sems.at[0])
    landed(scales_out, back_sems.at[1])


def unpack(codes, scales, surface, tracer_out, surface_out):
    for u in range(codes.shape[0]):
        values = decode(codes[u])
        for a in range(2):
            tracer_out[a, u] = values[a] * scales[pl.ds(a, 1), :]
    surface_out[...] = surface[...]


def local(
    tracer_adjoint,
    surface_adjoint,
    velocity,
    vertical_coupling,
    ocean_levels,
    face_conductance,
    buoyancy_weights,
    surface_flux,
):
    groups, tiles = lax.axis_size("grp"), lax.axis_size("tile")
    levels = vertical_coupling.shape[0]
    share = levels // tiles
    cells = (ROWS, LANES)
    blocks = 2 * UP + 1
    f32, i32 = jnp.float32, jnp.int32
    anywhere = pl.BlockSpec(memory_space=pl.ANY)
    vmem = pl.BlockSpec(memory_space=pltpu.VMEM)
    dma = pltpu.SemaphoreType.DMA
    packed = (tiles, share) + cells
    codes, scales, surface = pl.pallas_call(
        functools.partial(kernel, (groups, tiles, share, levels)),
        out_shape=(
            jax.ShapeDtypeStruct((share, ROWS, tiles * LANES), i32),
            jax.ShapeDtypeStruct((2, tiles * LANES), f32),
            jax.ShapeDtypeStruct(surface_adjoint.shape, f32),
        ),
        in_specs=[anywhere] * 8,
        out_specs=(anywhere, anywhere, vmem),
        scratch_shapes=[
            pltpu.VMEM(tracer_adjoint.shape, f32),
            pltpu.VMEM(cells, f32),
            pltpu.VMEM(vertical_coupling.shape, f32),
            pltpu.VMEM(cells, i32),
            pltpu.VMEM((4,) + cells, f32),
            pltpu.SMEM(buoyancy_weights.shape, f32),
            pltpu.SMEM(surface_flux.shape, f32),
            pltpu.VMEM(packed, i32),
            pltpu.VMEM((tiles, 2, LANES), f32),
            pltpu.VMEM(packed, i32),
            pltpu.VMEM((tiles, 2, LANES), f32),
            pltpu.VMEM((2, levels) + cells, jnp.bfloat16),
            pltpu.VMEM(packed, i32),
            pltpu.VMEM((tiles, 2, LANES), f32),
            pltpu.VMEM((FIELDS,) + cells, f32),
            pltpu.VMEM(cells, f32),
            pltpu.VMEM((blocks - 1, FIELDS) + cells, f32),
            pltpu.VMEM((blocks, 2) + cells, f32),
            pltpu.VMEM((3 * blocks - 1,) + cells, f32),
            pltpu.VMEM((FIELDS, HIGH, 2 * LANES), f32),
            pltpu.VMEM((4, HIGH, 2 * LANES), f32),
            pltpu.VMEM((levels,) + cells, f32),
            pltpu.VMEM((levels,) + cells, f32),
            pltpu.VMEM((levels,) + cells, f32),
            pltpu.VMEM((2, levels) + cells, f32),
            pltpu.VMEM((2, levels) + cells, f32),
            pltpu.VMEM(cells, f32),
            pltpu.VMEM((1 + CHUNKS, 2, 2) + cells, f32),
            pltpu.VMEM((1 + CHUNKS, 2, 2) + cells, f32),
            pltpu.VMEM((STEPS, 2, CHUNKS, 2, levels // CHUNKS, LANES), f32),
            pltpu.VMEM((STEPS, 2, CHUNKS, 2, levels // CHUNKS, LANES), f32),
            dma((7,)),
            dma((tiles,)),
            dma((tiles,)),
            dma((tiles,)),
            dma((8,)),
            dma((2,)),
            dma((3,)),
            dma((1 + CHUNKS, 2, 2)),
            dma((1 + CHUNKS, 2, 2)),
        ],
        compiler_params=pltpu.CompilerParams(collective_id=0, has_side_effects=True),
    )(
        tracer_adjoint,
        surface_adjoint,
        velocity,
        vertical_coupling,
        ocean_levels,
        face_conductance,
        buoyancy_weights,
        surface_flux,
    )
    return pl.pallas_call(
        unpack,
        out_shape=(
            jax.ShapeDtypeStruct(tracer_adjoint.shape, f32),
            jax.ShapeDtypeStruct(surface_adjoint.shape, f32),
        ),
        in_specs=[vmem] * 3,
        out_specs=(vmem, vmem),
    )(codes, scales, surface)


def solution(mesh):
    in_specs = (
        P(None, "tile", "grp", None),
        P("grp", "tile"),
        P(None, "tile", "grp", None),
        P(None, "grp", "tile"),
        P("grp", "tile"),
        P(None, "grp", "tile"),
        P(),
        P(),
    )
    out_specs = (P(None, "tile", "grp", None), P("grp", "tile"))
    return jax.shard_map(local, mesh=mesh, in_specs=in_specs, out_specs=out_specs, check_vma=False)
```

```python
import functools

import jax
import jax.numpy as jnp
from jax import lax
from jax.experimental import pallas as pl
from jax.experimental.pallas import tpu as pltpu
from jax.sharding import PartitionSpec as P

SOLVE_ITERS = 12
STEPS = 2
DIFFUSION = 0.1
CODE_MAX = 32767.0
MESH = pl.DeviceIdType.MESH
ROWS = 8
LANES = 128
UP = 2
HIGH = (2 * UP + 1) * ROWS
EDGE = 16
FIELDS = 4
QUAD = 4
CHUNKS = 2
EARLY = 8


def wrap(value, size):
    return lax.rem(value + 2 * size, size)


def push(src, dst, send_sem, recv_sem, device):
    return pltpu.make_async_remote_copy(
        src_ref=src,
        dst_ref=dst,
        send_sem=send_sem,
        recv_sem=recv_sem,
        device_id=device,
        device_id_type=MESH,
    )


def landed(ref, sem):
    pltpu.make_async_copy(ref, ref, sem).wait()


def lanes_of(i):
    return pl.ds(pl.multiple_of(i * LANES, LANES), LANES)


def decode(word):
    first = lax.shift_right_arithmetic(word + 32768, 16)
    second = word - lax.shift_left(first, 16)
    return (first.astype(jnp.float32), second.astype(jnp.float32))


def kernel(
    sizes,
    tracer_in,
    surface_in,
    velocity,
    coupling_in,
    ocean_levels,
    conductance_in,
    weights_in,
    flux_in,
    codes_out,
    scales_out,
    surface_out,
    tracer,
    surface,
    coupling,
    depths,
    conductance,
    weights,
    flux,
    sent_codes,
    sent_scales,
    codes,
    scales,
    currents,
    back_codes,
    back_scales,
    mine,
    mine_edge,
    middle,
    sides,
    around,
    fields,
    folded,
    inverse,
    lower,
    forward,
    grad,
    partial,
    surf_block,
    lane_send,
    lane_recv,
    row_send,
    row_recv,
    load_sems,
    code_sems,
    scale_sems,
    current_sems,
    send_sems,
    back_sems,
    near_sems,
    lane_sems,
    row_sems,
):
    groups, tiles, share, levels = sizes
    quads = tiles // QUAD
    deep = QUAD * share
    group = lax.axis_index("grp")
    tile = lax.axis_index("tile")
    def near_device(a, b):
        return (group - (a - UP), wrap(tile - (b - 1), tiles))

    above = [(group + a >= 0) & (group + a < groups) for a in range(-UP, UP + 1)]
    below = above[::-1]

    def where_present(present, action):
        for a in range(2 * UP + 1):
            if a == UP:
                action(a)
            else:
                pl.when(present[a])(functools.partial(action, a))

    loads = [
        pltpu.make_async_copy(src, dst, load_sems.at[n])
        for n, (src, dst) in enumerate(
            [
                (tracer_in, tracer),
                (conductance_in, conductance),
                (surface_in, surface),
                (ocean_levels, depths),
                (coupling_in, coupling),
                (weights_in, weights),
                (flux_in, flux),
            ]
        )
    ]
    loads[0].start()

    barrier = pltpu.get_barrier_semaphore()

    def greet(i, _):
        pl.semaphore_signal(
            barrier, inc=1, device_id=(group, wrap(tile + i, tiles)), device_id_type=MESH
        )
        return 0

    lax.fori_loop(1, tiles, greet, 0)

    def greet_rows(a):
        for b in range(3):
            if a != UP:
                pl.semaphore_signal(
                    barrier, inc=1, device_id=near_device(a, b), device_id_type=MESH
                )

    where_present(below, greet_rows)
    for load in loads[1:]:
        load.start()

    rows_near = 0
    for a in range(1, UP + 1):
        rows_near += (group + groups - a) // groups + (2 * groups - 1 - group - a) // groups
    pl.semaphore_wait(barrier, tiles - 1 + 3 * rows_near)

    def others(action, first=1, last=tiles):
        def one(i, _):
            action(wrap(tile + i, tiles))
            return 0

        lax.fori_loop(first, last, one, 0)

    def send_current(to):
        push(
            velocity.at[:, :, :, lanes_of(to)],
            currents.at[:, pl.ds(tile * share, share)],
            send_sems.at[0],
            current_sems.at[tile],
            (group, to),
        ).start()

    others(send_current, 1, 1 + EARLY)
    pltpu.make_async_copy(
        velocity.at[:, :, :, lanes_of(tile)],
        currents.at[:, pl.ds(tile * share, share)],
        current_sems.at[tile],
    ).start()

    lane = lax.broadcasted_iota(jnp.int32, (ROWS, LANES), 1)
    row = lax.broadcasted_iota(jnp.int32, (ROWS, LANES), 0)
    loads[1].wait()
    loads[2].wait()
    own = [
        conductance[0],
        conductance[2],
        1.0 / (1.0 + conductance[0] + conductance[1] + conductance[2] + conductance[3]),
        surface[...],
    ]
    packed = own[0]
    for f in range(FIELDS):
        mine[f] = own[f]
        western = own[f] if f == 0 else pltpu.roll(own[f], EDGE * f, 1)
        eastern = pltpu.roll(own[f], LANES // 2 + EDGE * (f + 1), 1)
        packed = jnp.where((lane >= EDGE * f) & (lane < EDGE * (f + 1)), western, packed)
        packed = jnp.where(
            (lane >= LANES // 2 + EDGE * f) & (lane < LANES // 2 + EDGE * (f + 1)), eastern, packed
        )
    mine_edge[...] = packed

    def encode(values, slot, code_ref, scale_ref):
        rounded = []
        for a in range(2):
            peak = functools.reduce(jnp.maximum, [jnp.abs(v) for v in values[a]])
            peak = jnp.maximum(jnp.max(peak, axis=0, keepdims=True), 1e-30)
            gain = jnp.broadcast_to(CODE_MAX / peak, (ROWS, LANES))
            scale_ref[slot, pl.ds(a, 1), :] = peak * (1.0 / CODE_MAX)
            rounded.append([jnp.floor(v * gain + 0.5).astype(jnp.int32) for v in values[a]])
        for u in range(share):
            code_ref[slot, u] = lax.shift_left(rounded[0][u], 16) + rounded[1][u]

    loads[0].wait()

    def encode_tracer(to, _):
        values = [[tracer[a, u, :, lanes_of(to)] for u in range(share)] for a in range(2)]
        encode(values, to, sent_codes, sent_scales)
        return 0

    lax.fori_loop(0, tiles, encode_tracer, 0)

    def middle_slot(a):
        return a if a < UP else a - 1

    def send_fields(a):
        for b in range(3):
            if b != 1:
                push(
                    mine_edge,
                    sides.at[a, b // 2],
                    near_sems.at[1, 0, a],
                    near_sems.at[1, 1, a],
                    near_device(a, b),
                ).start()
            elif a != UP:
                push(
                    mine,
                    middle.at[middle_slot(a)],
                    near_sems.at[0, 0, a],
                    near_sems.at[0, 1, a],
                    near_device(a, b),
                ).start()

    def fields_passed(a, way):
        landed(sides.at[a], near_sems.at[1, way, a])
        if a != UP:
            landed(middle.at[middle_slot(a)], near_sems.at[0, way, a])

    def send_around(a):
        for b in range(3):
            if (a, b) != (UP, 1):
                push(
                    surf_block,
                    around.at[a, b],
                    near_sems.at[2, 0, a],
                    near_sems.at[2, 1, a],
                    near_device(a, b),
                ).start()

    def around_passed(a, way):
        blocks = around.at[a, pl.ds(0, 2)] if a == UP else around.at[a]
        landed(blocks, near_sems.at[2, way, a])

    where_present(below, send_fields)

    def send_codes(to):
        push(
            sent_codes.at[to], codes.at[tile], send_sems.at[1], code_sems.at[tile], (group, to)
        ).start()
        push(
            sent_scales.at[to], scales.at[tile], send_sems.at[2], scale_sems.at[tile], (group, to)
        ).start()

    others(send_codes)
    pltpu.make_async_copy(sent_codes.at[tile], codes.at[tile], code_sems.at[tile]).start()
    pltpu.make_async_copy(sent_scales.at[tile], scales.at[tile], scale_sems.at[tile]).start()
    others(send_current, 1 + EARLY, tiles)
    for load in loads[3:]:
        load.wait()
    depth = depths[...]

    def factor(k, carry):
        previous, level_coup = carry
        following = jnp.where(k + 1 < depth, coupling[jnp.minimum(k + 1, levels - 1)], 0.0)
        diagonal = 1.0 + level_coup + following
        reciprocal = 1.0 / (diagonal - level_coup * previous)
        ahead = following * reciprocal
        inverse[k] = reciprocal
        lower[k] = level_coup * reciprocal
        forward[k] = ahead
        return (ahead, following)

    nothing = jnp.zeros((ROWS, LANES), jnp.float32)
    lax.fori_loop(0, levels, factor, (nothing, nothing))

    east_lanes = lane < EDGE
    side_inside = (east_lanes & (tile < tiles - 1)) | ((lane >= LANES - EDGE) & (tile > 0))

    def place(f, a, middle_block, side_block):
        rows = pl.ds(a * ROWS, ROWS)
        fields[f, rows, pl.ds(0, LANES)] = jnp.where(above[a], middle_block, 0.0)
        fields[f, rows, pl.ds(LANES, LANES)] = jnp.where(
            side_inside & above[a], side_block, 0.0
        )

    where_present(above, lambda a: fields_passed(a, 1))
    for a in range(2 * UP + 1):
        from_west, from_east = sides[a, 0], sides[a, 1]
        for f in range(FIELDS):
            east = from_east if f == 0 else pltpu.roll(from_east, LANES - EDGE * f, 1)
            west = pltpu.roll(from_west, (LANES // 2 - EDGE * (f + 1)) % LANES, 1)
            place(
                f,
                a,
                mine[f] if a == UP else middle[middle_slot(a), f],
                jnp.where(east_lanes, east, west),
            )
    eastern, northern, region_recip = fields[0], fields[1], fields[2]
    folded[0] = eastern * region_recip
    folded[1] = pltpu.roll(eastern, 1, 1) * region_recip
    folded[2] = northern * region_recip
    folded[3] = pltpu.roll(northern, 1, 0) * region_recip

    def relax():
        source = fields[FIELDS - 1]
        scaled = source * fields[2]

        def sweep(_, iterate):
            return (
                scaled
                + folded[0] * pltpu.roll(iterate, 2 * LANES - 1, 1)
                + folded[1] * pltpu.roll(iterate, 1, 1)
                + folded[2] * pltpu.roll(iterate, HIGH - 1, 0)
                + folded[3] * pltpu.roll(iterate, 1, 0)
            )

        solved = lax.fori_loop(0, SOLVE_ITERS, sweep, source)
        return solved[UP * ROWS : (UP + 1) * ROWS, :LANES]

    def downward(k, sources, relaxed, carry):
        wet = jnp.where(k < depth, relaxed, 0.0)
        level_inv, level_low = inverse[k], lower[k]
        done = []
        for a in range(2):
            current = (sources[a] + weights[a, k] * wet) * level_inv + level_low * carry[a]
            grad[a, k] = current
            done.append(current)
        return tuple(done)

    def upward():
        def rise(j, carry):
            for u in range(deep):
                k = levels - 1 - (j * deep + u)
                ahead = forward[k]
                wet = k < depth
                carry = tuple(grad[a, k] + ahead * carry[a] for a in range(2))
                for a in range(2):
                    grad[a, k] = jnp.where(wet, carry[a], 0.0)
            return carry

        return lax.fori_loop(0, quads, rise, (nothing, nothing))

    def next_surface(relaxed, top):
        return relaxed + jnp.where(0 < depth, flux[0] * top[0] + flux[1] * top[1], 0.0)

    def row_place(quad, u):
        return (lax.rem(quad, CHUNKS), lax.div(quad, CHUNKS) * deep + u)

    def give(step, quad, carry):
        carry = list(carry)
        for u in range(deep):
            k = quad * deep + u
            chunk, place_at = row_place(quad, u)
            zonal = 0.5 * currents[0, k].astype(jnp.float32)
            meridional = 0.5 * currents[1, k].astype(jnp.float32)
            for a in range(2):
                masked = grad[a, k]
                westward = masked * (DIFFUSION + zonal)
                eastward = masked * (DIFFUSION - zonal)
                southward = masked * (DIFFUSION + meridional)
                northward = pltpu.roll(masked * (DIFFUSION - meridional), 1, 0)
                partial[a, k] = (
                    (1.0 - 4.0 * DIFFUSION) * masked
                    + jnp.where(lane == LANES - 1, 0.0, pltpu.roll(westward, LANES - 1, 1))
                    + jnp.where(lane == 0, 0.0, pltpu.roll(eastward, 1, 1))
                    + jnp.where(row == ROWS - 1, 0.0, pltpu.roll(southward, ROWS - 1, 0))
                    + jnp.where(row == 0, 0.0, northward)
                )
                at_level = lane == k
                carry[2 * a] = jnp.where(at_level, pltpu.roll(westward, k, 1), carry[2 * a])
                carry[2 * a + 1] = jnp.where(
                    at_level, pltpu.roll(eastward, k + 1, 1), carry[2 * a + 1]
                )
                row_send[step, 0, chunk, a, pl.ds(place_at, 1), :] = southward[0:1]
                row_send[step, 1, chunk, a, pl.ds(place_at, 1), :] = northward[0:1]
        return tuple(carry)

    def keep_edges(message, edges):
        for a in range(2):
            for side in range(2):
                lane_send[message, side, a] = edges[2 * a + side]

    def edge_copies(way, step, chunk=None):
        message = 0 if chunk is None else 1 + chunk
        copies = []
        for side in range(2):
            rows = [ref.at[step, side] for ref in (row_send, row_recv)]
            if chunk is not None:
                rows = [ref.at[chunk] for ref in rows]
            southern, northern = group > 0, group < groups - 1
            copies += [
                (
                    (southern, northern)[side if way == 0 else 1 - side],
                    push(
                        rows[0],
                        rows[1],
                        row_sems.at[message, 0, side],
                        row_sems.at[message, 1, side],
                        (group - 1 + 2 * side, tile),
                    ),
                ),
                (
                    group >= 0,
                    push(
                        lane_send.at[message, side],
                        lane_recv.at[message, side],
                        lane_sems.at[message, 0, side],
                        lane_sems.at[message, 1, side],
                        (group, wrap(tile - 1 + 2 * side, tiles)),
                    ),
                ),
            ]
        return copies

    at_east = (lane == LANES - 1) & (tile < tiles - 1)
    at_west = (lane == 0) & (tile > 0)
    at_north = (row == ROWS - 1) & (group < groups - 1)
    at_south = (row == 0) & (group > 0)

    def gathered(step, message, a, quad, u):
        k = quad * deep + u
        chunk, place_at = row_place(quad, u)
        east = pltpu.roll(lane_recv[message, 0, a], LANES - 1 - k, 1)
        west = pltpu.roll(lane_recv[message, 1, a], LANES - k, 1)
        north = row_recv[step, 0, chunk, a, pl.ds(place_at, 1), :]
        south = row_recv[step, 1, chunk, a, pl.ds(place_at, 1), :]
        return (
            partial[a, k]
            + jnp.where(at_east, east, 0.0)
            + jnp.where(at_west, west, 0.0)
            + jnp.where(at_north, jnp.broadcast_to(north, (ROWS, LANES)), 0.0)
            + jnp.where(at_south, jnp.broadcast_to(south, (ROWS, LANES)), 0.0)
        )

    relaxed = relax()

    def first_down(s, carry):
        landed(codes.at[s], code_sems.at[s])
        landed(scales.at[s], scale_sems.at[s])
        factors = [scales[s, pl.ds(a, 1), :] for a in range(2)]
        for u in range(share):
            k = s * share + u
            values = decode(codes[s, u])
            carry = downward(k, [values[a] * factors[a] for a in range(2)], relaxed, carry)
        return carry

    lax.fori_loop(0, tiles, first_down, (nothing, nothing))
    top = upward()
    surf_block[...] = next_surface(relaxed, top)

    def arrived_give(i, carry):
        quad = wrap(lax.div(tile, QUAD) - i, quads)
        for v in range(QUAD):
            s = quad * QUAD + v
            landed(currents.at[:, pl.ds(s * share, share)], current_sems.at[s])
        return give(0, quad, carry)

    edges = arrived_give(0, (nothing,) * 4)
    where_present(below, send_around)
    edges = lax.fori_loop(1, quads, arrived_give, edges)
    keep_edges(0, edges)

    for present, copy in edge_copies(0, 0):
        pl.when(present)(copy.start)
    where_present(above, lambda a: around_passed(a, 1))
    for a in range(2 * UP + 1):
        blocks = [surf_block if (a, b) == (UP, 1) else around.at[a, b] for b in range(3)]
        place(FIELDS - 1, a, blocks[1][...], jnp.where(east_lanes, blocks[2][...], blocks[0][...]))
    relaxed_again = relax()
    for present, copy in edge_copies(1, 0):
        pl.when(present)(copy.wait_recv)

    def second_down(quad, carry):
        for u in range(deep):
            sources = [gathered(0, 0, a, quad, u) for a in range(2)]
            carry = downward(quad * deep + u, sources, relaxed_again, carry)
        return carry

    lax.fori_loop(0, quads, second_down, (nothing, nothing))
    top = upward()
    surface_out[...] = next_surface(relaxed_again, top)

    turn = lax.div(lax.div(tile, QUAD), CHUNKS)

    def quad_of(chunk, i):
        return wrap(turn - i, quads // CHUNKS) * CHUNKS + chunk

    for chunk in range(CHUNKS):
        edges = lax.fori_loop(
            0,
            quads // CHUNKS,
            lambda i, carry, chunk=chunk: give(1, quad_of(chunk, i), carry),
            (nothing,) * 4,
        )
        keep_edges(1 + chunk, edges)
        for present, copy in edge_copies(0, 1, chunk):
            pl.when(present)(copy.start)

    landed(currents.at[:, pl.ds(0, levels - share)], send_sems.at[0])
    landed(sent_codes.at[pl.ds(0, tiles - 1)], send_sems.at[1])
    landed(sent_scales.at[pl.ds(0, tiles - 1)], send_sems.at[2])

    def near_sent(a):
        fields_passed(a, 0)
        around_passed(a, 0)

    where_present(below, near_sent)
    for present, copy in edge_copies(0, 0):
        pl.when(present)(copy.wait_send)

    def back_refs(to):
        return [
            (back_codes.at[to], codes_out.at[:, :, lanes_of(tile)], 0),
            (back_scales.at[to], scales_out.at[:, lanes_of(tile)], 1),
        ]

    def send_back(quad):
        for v in range(QUAD):
            to = quad * QUAD + v

            @pl.when(to != tile)
            def _():
                for src, dst, n in back_refs(to):
                    push(src, dst, send_sems.at[3 + n], back_sems.at[n], (group, to)).start()

    for chunk in range(CHUNKS):
        for present, copy in edge_copies(1, 1, chunk):
            pl.when(present)(copy.wait_recv)

        def finish(i, _, chunk=chunk):
            quad = quad_of(chunk, i)
            for v in range(QUAD):
                values = [
                    [gathered(1, 1 + chunk, a, quad, v * share + u) for u in range(share)]
                    for a in range(2)
                ]
                encode(values, quad * QUAD + v, back_codes, back_scales)

            @pl.when(i > 0)
            def _():
                send_back(quad_of(chunk, i - 1))

            return 0

        lax.fori_loop(0, quads // CHUNKS, finish, 0)
        send_back(quad_of(chunk, quads // CHUNKS - 1))
    for src, dst, n in back_refs(tile):
        pltpu.make_async_copy(src, dst, back_sems.at[n]).start()

    for chunk in range(CHUNKS):
        for present, copy in edge_copies(0, 1, chunk):
            pl.when(present)(copy.wait_send)
    landed(back_codes.at[pl.ds(0, tiles - 1)], send_sems.at[3])
    landed(back_scales.at[pl.ds(0, tiles - 1)], send_sems.at[4])
    landed(codes_out, back_sems.at[0])
    landed(scales_out, back_sems.at[1])


def unpack(codes, scales, surface, tracer_out, surface_out):
    for u in range(codes.shape[0]):
        values = decode(codes[u])
        for a in range(2):
            tracer_out[a, u] = values[a] * scales[pl.ds(a, 1), :]
    surface_out[...] = surface[...]


def local(
    tracer_adjoint,
    surface_adjoint,
    velocity,
    vertical_coupling,
    ocean_levels,
    face_conductance,
    buoyancy_weights,
    surface_flux,
):
    groups, tiles = lax.axis_size("grp"), lax.axis_size("tile")
    levels = vertical_coupling.shape[0]
    share = levels // tiles
    cells = (ROWS, LANES)
    blocks = 2 * UP + 1
    f32, i32 = jnp.float32, jnp.int32
    anywhere = pl.BlockSpec(memory_space=pl.ANY)
    vmem = pl.BlockSpec(memory_space=pltpu.VMEM)
    dma = pltpu.SemaphoreType.DMA
    packed = (tiles, share) + cells
    codes, scales, surface = pl.pallas_call(
        functools.partial(kernel, (groups, tiles, share, levels)),
        out_shape=(
            jax.ShapeDtypeStruct((share, ROWS, tiles * LANES), i32),
            jax.ShapeDtypeStruct((2, tiles * LANES), f32),
            jax.ShapeDtypeStruct(surface_adjoint.shape, f32),
        ),
        in_specs=[anywhere] * 8,
        out_specs=(anywhere, anywhere, vmem),
        scratch_shapes=[
            pltpu.VMEM(tracer_adjoint.shape, f32),
            pltpu.VMEM(cells, f32),
            pltpu.VMEM(vertical_coupling.shape, f32),
            pltpu.VMEM(cells, i32),
            pltpu.VMEM((4,) + cells, f32),
            pltpu.SMEM(buoyancy_weights.shape, f32),
            pltpu.SMEM(surface_flux.shape, f32),
            pltpu.VMEM(packed, i32),
            pltpu.VMEM((tiles, 2, LANES), f32),
            pltpu.VMEM(packed, i32),
            pltpu.VMEM((tiles, 2, LANES), f32),
            pltpu.VMEM((2, levels) + cells, jnp.bfloat16),
            pltpu.VMEM(packed, i32),
            pltpu.VMEM((tiles, 2, LANES), f32),
            pltpu.VMEM((FIELDS,) + cells, f32),
            pltpu.VMEM(cells, f32),
            pltpu.VMEM((blocks - 1, FIELDS) + cells, f32),
            pltpu.VMEM((blocks, 2) + cells, f32),
            pltpu.VMEM((blocks, 3) + cells, f32),
            pltpu.VMEM((FIELDS, HIGH, 2 * LANES), f32),
            pltpu.VMEM((4, HIGH, 2 * LANES), f32),
            pltpu.VMEM((levels,) + cells, f32),
            pltpu.VMEM((levels,) + cells, f32),
            pltpu.VMEM((levels,) + cells, f32),
            pltpu.VMEM((2, levels) + cells, f32),
            pltpu.VMEM((2, levels) + cells, f32),
            pltpu.VMEM(cells, f32),
            pltpu.VMEM((1 + CHUNKS, 2, 2) + cells, f32),
            pltpu.VMEM((1 + CHUNKS, 2, 2) + cells, f32),
            pltpu.VMEM((STEPS, 2, CHUNKS, 2, levels // CHUNKS, LANES), f32),
            pltpu.VMEM((STEPS, 2, CHUNKS, 2, levels // CHUNKS, LANES), f32),
            dma((7,)),
            dma((tiles,)),
            dma((tiles,)),
            dma((tiles,)),
            dma((5,)),
            dma((2,)),
            dma((3, 2, blocks)),
            dma((1 + CHUNKS, 2, 2)),
            dma((1 + CHUNKS, 2, 2)),
        ],
        compiler_params=pltpu.CompilerParams(collective_id=0, has_side_effects=True),
    )(
        tracer_adjoint,
        surface_adjoint,
        velocity,
        vertical_coupling,
        ocean_levels,
        face_conductance,
        buoyancy_weights,
        surface_flux,
    )
    return pl.pallas_call(
        unpack,
        out_shape=(
            jax.ShapeDtypeStruct(tracer_adjoint.shape, f32),
            jax.ShapeDtypeStruct(surface_adjoint.shape, f32),
        ),
        in_specs=[vmem] * 3,
        out_specs=(vmem, vmem),
    )(codes, scales, surface)


def solution(mesh):
    in_specs = (
        P(None, "tile", "grp", None),
        P("grp", "tile"),
        P(None, "tile", "grp", None),
        P(None, "grp", "tile"),
        P("grp", "tile"),
        P(None, "grp", "tile"),
        P(),
        P(),
    )
    out_specs = (P(None, "tile", "grp", None), P("grp", "tile"))
    return jax.shard_map(local, mesh=mesh, in_specs=in_specs, out_specs=out_specs, check_vma=False)
```

```python
import functools

import jax
import jax.numpy as jnp
from jax import lax
from jax.experimental import pallas as pl
from jax.experimental.pallas import tpu as pltpu
from jax.sharding import PartitionSpec as P

SOLVE_ITERS = 12
STEPS = 2
DIFFUSION = 0.1
CODE_MAX = 32767.0
MESH = pl.DeviceIdType.MESH
ROWS = 8
LANES = 128
UP = 2
HIGH = (2 * UP + 1) * ROWS
EDGE = 16
FIELDS = 4
QUAD = 4
CHUNKS = 2
EARLY = 8


def wrap(value, size):
    return lax.rem(value + 2 * size, size)


def push(src, dst, send_sem, recv_sem, device):
    return pltpu.make_async_remote_copy(
        src_ref=src,
        dst_ref=dst,
        send_sem=send_sem,
        recv_sem=recv_sem,
        device_id=device,
        device_id_type=MESH,
    )


def landed(ref, sem):
    pltpu.make_async_copy(ref, ref, sem).wait()


def lanes_of(i):
    return pl.ds(pl.multiple_of(i * LANES, LANES), LANES)


def decode(word):
    first = lax.shift_right_arithmetic(word + 32768, 16)
    second = word - lax.shift_left(first, 16)
    return (first.astype(jnp.float32), second.astype(jnp.float32))


def kernel(
    sizes,
    tracer_in,
    surface_in,
    velocity,
    coupling_in,
    ocean_levels,
    conductance_in,
    weights_in,
    flux_in,
    codes_out,
    scales_out,
    surface_out,
    tracer,
    surface,
    coupling,
    depths,
    conductance,
    weights,
    flux,
    sent_codes,
    sent_scales,
    codes,
    scales,
    currents,
    back_codes,
    back_scales,
    mine,
    mine_edge,
    middle,
    sides,
    around,
    fields,
    folded,
    inverse,
    lower,
    forward,
    grad,
    partial,
    surf_block,
    lane_send,
    lane_recv,
    row_send,
    row_recv,
    load_sems,
    code_sems,
    scale_sems,
    current_sems,
    send_sems,
    back_sems,
    near_sems,
    lane_sems,
    row_sems,
):
    groups, tiles, share, levels = sizes
    quads = tiles // QUAD
    deep = QUAD * share
    group = lax.axis_index("grp")
    tile = lax.axis_index("tile")
    def near_device(a, b):
        return (group - (a - UP), wrap(tile - (b - 1), tiles))

    above = [(group + a >= 0) & (group + a < groups) for a in range(-UP, UP + 1)]
    below = above[::-1]

    def where_present(present, action):
        for a in range(2 * UP + 1):
            if a == UP:
                action(a)
            else:
                pl.when(present[a])(functools.partial(action, a))

    loads = [
        pltpu.make_async_copy(src, dst, load_sems.at[n])
        for n, (src, dst) in enumerate(
            [
                (tracer_in, tracer),
                (conductance_in, conductance),
                (surface_in, surface),
                (ocean_levels, depths),
                (coupling_in, coupling),
                (weights_in, weights),
                (flux_in, flux),
            ]
        )
    ]
    loads[0].start()

    barrier = pltpu.get_barrier_semaphore()

    for i in range(1, tiles):
        pl.semaphore_signal(
            barrier, inc=1, device_id=(group, wrap(tile + i, tiles)), device_id_type=MESH
        )

    def greet_rows(a):
        for b in range(3):
            if a != UP:
                pl.semaphore_signal(
                    barrier, inc=1, device_id=near_device(a, b), device_id_type=MESH
                )

    where_present(below, greet_rows)
    for load in loads[1:]:
        load.start()

    rows_near = 0
    for a in range(1, UP + 1):
        rows_near += (group + groups - a) // groups + (2 * groups - 1 - group - a) // groups
    pl.semaphore_wait(barrier, tiles - 1 + 3 * rows_near)

    def others(action, first=1, last=tiles):
        def one(i, _):
            action(wrap(tile + i, tiles))
            return 0

        lax.fori_loop(first, last, one, 0)

    def send_current(to):
        push(
            velocity.at[:, :, :, lanes_of(to)],
            currents.at[:, pl.ds(tile * share, share)],
            send_sems.at[0],
            current_sems.at[tile],
            (group, to),
        ).start()

    others(send_current, 1, 1 + EARLY)
    pltpu.make_async_copy(
        velocity.at[:, :, :, lanes_of(tile)],
        currents.at[:, pl.ds(tile * share, share)],
        current_sems.at[tile],
    ).start()

    lane = lax.broadcasted_iota(jnp.int32, (ROWS, LANES), 1)
    row = lax.broadcasted_iota(jnp.int32, (ROWS, LANES), 0)
    loads[1].wait()
    loads[2].wait()
    own = [
        conductance[0],
        conductance[2],
        1.0 / (1.0 + conductance[0] + conductance[1] + conductance[2] + conductance[3]),
        surface[...],
    ]
    packed = own[0]
    for f in range(FIELDS):
        mine[f] = own[f]
        western = own[f] if f == 0 else pltpu.roll(own[f], EDGE * f, 1)
        eastern = pltpu.roll(own[f], LANES // 2 + EDGE * (f + 1), 1)
        packed = jnp.where((lane >= EDGE * f) & (lane < EDGE * (f + 1)), western, packed)
        packed = jnp.where(
            (lane >= LANES // 2 + EDGE * f) & (lane < LANES // 2 + EDGE * (f + 1)), eastern, packed
        )
    mine_edge[...] = packed

    def encode(values, slot, code_ref, scale_ref):
        rounded = []
        for a in range(2):
            peak = functools.reduce(jnp.maximum, [jnp.abs(v) for v in values[a]])
            peak = jnp.maximum(jnp.max(peak, axis=0, keepdims=True), 1e-30)
            gain = jnp.broadcast_to(CODE_MAX / peak, (ROWS, LANES))
            scale_ref[slot, pl.ds(a, 1), :] = peak * (1.0 / CODE_MAX)
            rounded.append([jnp.floor(v * gain + 0.5).astype(jnp.int32) for v in values[a]])
        for u in range(share):
            code_ref[slot, u] = lax.shift_left(rounded[0][u], 16) + rounded[1][u]

    loads[0].wait()

    def encode_tracer(to, _):
        values = [[tracer[a, u, :, lanes_of(to)] for u in range(share)] for a in range(2)]
        encode(values, to, sent_codes, sent_scales)
        return 0

    lax.fori_loop(0, tiles, encode_tracer, 0)

    def middle_slot(a):
        return a if a < UP else a - 1

    def send_fields(a):
        for b in range(3):
            if b != 1:
                push(
                    mine_edge,
                    sides.at[a, b // 2],
                    near_sems.at[1, 0, a],
                    near_sems.at[1, 1, a],
                    near_device(a, b),
                ).start()
            elif a != UP:
                push(
                    mine,
                    middle.at[middle_slot(a)],
                    near_sems.at[0, 0, a],
                    near_sems.at[0, 1, a],
                    near_device(a, b),
                ).start()

    def fields_passed(a, way):
        landed(sides.at[a], near_sems.at[1, way, a])
        if a != UP:
            landed(middle.at[middle_slot(a)], near_sems.at[0, way, a])

    def send_around(a):
        for b in range(3):
            if (a, b) != (UP, 1):
                push(
                    surf_block,
                    around.at[a, b],
                    near_sems.at[2, 0, a],
                    near_sems.at[2, 1, a],
                    near_device(a, b),
                ).start()

    def around_passed(a, way):
        blocks = around.at[a, pl.ds(0, 2)] if a == UP else around.at[a]
        landed(blocks, near_sems.at[2, way, a])

    where_present(below, send_fields)

    def send_codes(to):
        push(
            sent_codes.at[to], codes.at[tile], send_sems.at[1], code_sems.at[tile], (group, to)
        ).start()
        push(
            sent_scales.at[to], scales.at[tile], send_sems.at[2], scale_sems.at[tile], (group, to)
        ).start()

    others(send_codes)
    pltpu.make_async_copy(sent_codes.at[tile], codes.at[tile], code_sems.at[tile]).start()
    pltpu.make_async_copy(sent_scales.at[tile], scales.at[tile], scale_sems.at[tile]).start()
    others(send_current, 1 + EARLY, tiles)
    for load in loads[3:]:
        load.wait()
    depth = depths[...]

    def factor(k, carry):
        previous, level_coup = carry
        following = jnp.where(k + 1 < depth, coupling[jnp.minimum(k + 1, levels - 1)], 0.0)
        diagonal = 1.0 + level_coup + following
        reciprocal = 1.0 / (diagonal - level_coup * previous)
        ahead = following * reciprocal
        inverse[k] = reciprocal
        lower[k] = level_coup * reciprocal
        forward[k] = ahead
        return (ahead, following)

    nothing = jnp.zeros((ROWS, LANES), jnp.float32)
    lax.fori_loop(0, levels, factor, (nothing, nothing))

    east_lanes = lane < EDGE
    side_inside = (east_lanes & (tile < tiles - 1)) | ((lane >= LANES - EDGE) & (tile > 0))

    def place(f, a, middle_block, side_block):
        rows = pl.ds(a * ROWS, ROWS)
        fields[f, rows, pl.ds(0, LANES)] = jnp.where(above[a], middle_block, 0.0)
        fields[f, rows, pl.ds(LANES, LANES)] = jnp.where(
            side_inside & above[a], side_block, 0.0
        )

    where_present(above, lambda a: fields_passed(a, 1))
    for a in range(2 * UP + 1):
        from_west, from_east = sides[a, 0], sides[a, 1]
        for f in range(FIELDS):
            east = from_east if f == 0 else pltpu.roll(from_east, LANES - EDGE * f, 1)
            west = pltpu.roll(from_west, (LANES // 2 - EDGE * (f + 1)) % LANES, 1)
            place(
                f,
                a,
                mine[f] if a == UP else middle[middle_slot(a), f],
                jnp.where(east_lanes, east, west),
            )
    eastern, northern, region_recip = fields[0], fields[1], fields[2]
    folded[0] = eastern * region_recip
    folded[1] = pltpu.roll(eastern, 1, 1) * region_recip
    folded[2] = northern * region_recip
    folded[3] = pltpu.roll(northern, 1, 0) * region_recip

    def relax():
        source = fields[FIELDS - 1]
        scaled = source * fields[2]

        def sweep(_, iterate):
            return (
                scaled
                + folded[0] * pltpu.roll(iterate, 2 * LANES - 1, 1)
                + folded[1] * pltpu.roll(iterate, 1, 1)
                + folded[2] * pltpu.roll(iterate, HIGH - 1, 0)
                + folded[3] * pltpu.roll(iterate, 1, 0)
            )

        solved = lax.fori_loop(0, SOLVE_ITERS, sweep, source)
        return solved[UP * ROWS : (UP + 1) * ROWS, :LANES]

    def downward(k, sources, relaxed, carry):
        wet = jnp.where(k < depth, relaxed, 0.0)
        level_inv, level_low = inverse[k], lower[k]
        done = []
        for a in range(2):
            current = (sources[a] + weights[a, k] * wet) * level_inv + level_low * carry[a]
            grad[a, k] = current
            done.append(current)
        return tuple(done)

    def upward():
        def rise(j, carry):
            for u in range(deep):
                k = levels - 1 - (j * deep + u)
                ahead = forward[k]
                wet = k < depth
                carry = tuple(grad[a, k] + ahead * carry[a] for a in range(2))
                for a in range(2):
                    grad[a, k] = jnp.where(wet, carry[a], 0.0)
            return carry

        return lax.fori_loop(0, quads, rise, (nothing, nothing))

    def next_surface(relaxed, top):
        return relaxed + jnp.where(0 < depth, flux[0] * top[0] + flux[1] * top[1], 0.0)

    def row_place(quad):
        return (lax.rem(quad, CHUNKS), lax.div(quad, CHUNKS))

    southern, northern = group > 0, group < groups - 1

    def send_rows(step, message, quad, ready=None):
        chunk, half = row_place(quad)
        for side, present in enumerate((southern, northern)):
            copy = push(
                row_send.at[step, side, chunk, half],
                row_recv.at[step, side, chunk, half],
                row_sems.at[message, 0, side],
                row_sems.at[message, 1, side],
                (group - 1 + 2 * side, tile),
            )
            pl.when(present if ready is None else present & ready)(copy.start)

    def give(step, quad, carry):
        carry = list(carry)
        chunk, half = row_place(quad)
        for u in range(deep):
            k = quad * deep + u
            zonal = 0.5 * currents[0, k].astype(jnp.float32)
            meridional = 0.5 * currents[1, k].astype(jnp.float32)
            for a in range(2):
                masked = grad[a, k]
                westward = masked * (DIFFUSION + zonal)
                eastward = masked * (DIFFUSION - zonal)
                southward = masked * (DIFFUSION + meridional)
                northward = pltpu.roll(masked * (DIFFUSION - meridional), 1, 0)
                partial[a, k] = (
                    (1.0 - 4.0 * DIFFUSION) * masked
                    + jnp.where(lane == LANES - 1, 0.0, pltpu.roll(westward, LANES - 1, 1))
                    + jnp.where(lane == 0, 0.0, pltpu.roll(eastward, 1, 1))
                    + jnp.where(row == ROWS - 1, 0.0, pltpu.roll(southward, ROWS - 1, 0))
                    + jnp.where(row == 0, 0.0, northward)
                )
                at_level = lane == k
                carry[2 * a] = jnp.where(at_level, pltpu.roll(westward, k, 1), carry[2 * a])
                carry[2 * a + 1] = jnp.where(
                    at_level, pltpu.roll(eastward, k + 1, 1), carry[2 * a + 1]
                )
                at_row = pl.ds(a * deep + u, 1)
                row_send[step, 0, chunk, half, at_row, :] = southward[0:1]
                row_send[step, 1, chunk, half, at_row, :] = northward[0:1]
        return tuple(carry)

    def keep_edges(message, edges):
        for a in range(2):
            for side in range(2):
                lane_send[message, side, a] = edges[2 * a + side]

    def lane_copies(message):
        return [
            push(
                lane_send.at[message, side],
                lane_recv.at[message, side],
                lane_sems.at[message, 0, side],
                lane_sems.at[message, 1, side],
                (group, wrap(tile - 1 + 2 * side, tiles)),
            )
            for side in range(2)
        ]

    def rows_passed(way, step, message):
        for side in range(2):
            rows = row_recv.at[step, side]
            if step:
                rows = rows.at[message - 1]
            present = (southern, northern)[side if way == 0 else 1 - side]
            pl.when(present)(
                functools.partial(landed, rows, row_sems.at[message, way, side])
            )

    at_east = (lane == LANES - 1) & (tile < tiles - 1)
    at_west = (lane == 0) & (tile > 0)
    at_north = (row == ROWS - 1) & (group < groups - 1)
    at_south = (row == 0) & (group > 0)

    def gathered(step, message, a, quad, u):
        k = quad * deep + u
        chunk, half = row_place(quad)
        at_row = pl.ds(a * deep + u, 1)
        east = pltpu.roll(lane_recv[message, 0, a], LANES - 1 - k, 1)
        west = pltpu.roll(lane_recv[message, 1, a], LANES - k, 1)
        north = row_recv[step, 0, chunk, half, at_row, :]
        south = row_recv[step, 1, chunk, half, at_row, :]
        return (
            partial[a, k]
            + jnp.where(at_east, east, 0.0)
            + jnp.where(at_west, west, 0.0)
            + jnp.where(at_north, jnp.broadcast_to(north, (ROWS, LANES)), 0.0)
            + jnp.where(at_south, jnp.broadcast_to(south, (ROWS, LANES)), 0.0)
        )

    relaxed = relax()

    def first_down(s, carry):
        landed(codes.at[s], code_sems.at[s])
        landed(scales.at[s], scale_sems.at[s])
        factors = [scales[s, pl.ds(a, 1), :] for a in range(2)]
        for u in range(share):
            k = s * share + u
            values = decode(codes[s, u])
            carry = downward(k, [values[a] * factors[a] for a in range(2)], relaxed, carry)
        return carry

    lax.fori_loop(0, tiles, first_down, (nothing, nothing))
    top = upward()
    surf_block[...] = next_surface(relaxed, top)

    def arrived_quad(i):
        return wrap(lax.div(tile, QUAD) - i, quads)

    def arrived_give(i, carry):
        quad = arrived_quad(i)
        for v in range(QUAD):
            s = quad * QUAD + v
            landed(currents.at[:, pl.ds(s * share, share)], current_sems.at[s])
        return give(0, quad, carry)

    edges = arrived_give(0, (nothing,) * 4)
    where_present(below, send_around)

    def send_and_give(i, carry):
        send_rows(0, 0, arrived_quad(i - 1))
        return arrived_give(i, carry)

    edges = lax.fori_loop(1, quads, send_and_give, edges)
    keep_edges(0, edges)
    send_rows(0, 0, arrived_quad(quads - 1))

    for copy in lane_copies(0):
        copy.start()
    where_present(above, lambda a: around_passed(a, 1))
    for a in range(2 * UP + 1):
        blocks = [surf_block if (a, b) == (UP, 1) else around.at[a, b] for b in range(3)]
        place(FIELDS - 1, a, blocks[1][...], jnp.where(east_lanes, blocks[2][...], blocks[0][...]))
    relaxed_again = relax()
    for copy in lane_copies(0):
        copy.wait_recv()
    rows_passed(1, 0, 0)

    def second_down(quad, carry):
        for u in range(deep):
            sources = [gathered(0, 0, a, quad, u) for a in range(2)]
            carry = downward(quad * deep + u, sources, relaxed_again, carry)
        return carry

    lax.fori_loop(0, quads, second_down, (nothing, nothing))
    top = upward()
    surface_out[...] = next_surface(relaxed_again, top)

    turn = lax.div(lax.div(tile, QUAD), CHUNKS)

    def quad_of(chunk, i):
        return wrap(turn - i, quads // CHUNKS) * CHUNKS + chunk

    for chunk in range(CHUNKS):

        def give_and_send(i, carry, chunk=chunk):
            send_rows(1, 1 + chunk, quad_of(chunk, i - 1), i > 0)
            return give(1, quad_of(chunk, i), carry)

        edges = lax.fori_loop(0, quads // CHUNKS, give_and_send, (nothing,) * 4)
        keep_edges(1 + chunk, edges)
        send_rows(1, 1 + chunk, quad_of(chunk, quads // CHUNKS - 1))
        for copy in lane_copies(1 + chunk):
            copy.start()

    landed(currents.at[:, pl.ds(0, levels - share)], send_sems.at[0])
    landed(sent_codes.at[pl.ds(0, tiles - 1)], send_sems.at[1])
    landed(sent_scales.at[pl.ds(0, tiles - 1)], send_sems.at[2])

    def near_sent(a):
        fields_passed(a, 0)
        around_passed(a, 0)

    where_present(below, near_sent)
    for copy in lane_copies(0):
        copy.wait_send()
    rows_passed(0, 0, 0)

    def back_refs(to):
        return [
            (back_codes.at[to], codes_out.at[:, :, lanes_of(tile)], 0),
            (back_scales.at[to], scales_out.at[:, lanes_of(tile)], 1),
        ]

    def send_back(quad):
        for v in range(QUAD):
            to = quad * QUAD + v

            @pl.when(to != tile)
            def _():
                for src, dst, n in back_refs(to):
                    push(src, dst, send_sems.at[3 + n], back_sems.at[n], (group, to)).start()

    for chunk in range(CHUNKS):
        for copy in lane_copies(1 + chunk):
            copy.wait_recv()
        rows_passed(1, 1, 1 + chunk)

        def finish(i, _, chunk=chunk):
            quad = quad_of(chunk, i)
            for v in range(QUAD):
                values = [
                    [gathered(1, 1 + chunk, a, quad, v * share + u) for u in range(share)]
                    for a in range(2)
                ]
                encode(values, quad * QUAD + v, back_codes, back_scales)

            @pl.when(i > 0)
            def _():
                send_back(quad_of(chunk, i - 1))

            return 0

        lax.fori_loop(0, quads // CHUNKS, finish, 0)
        send_back(quad_of(chunk, quads // CHUNKS - 1))
    for src, dst, n in back_refs(tile):
        pltpu.make_async_copy(src, dst, back_sems.at[n]).start()

    for chunk in range(CHUNKS):
        for copy in lane_copies(1 + chunk):
            copy.wait_send()
        rows_passed(0, 1, 1 + chunk)
    landed(back_codes.at[pl.ds(0, tiles - 1)], send_sems.at[3])
    landed(back_scales.at[pl.ds(0, tiles - 1)], send_sems.at[4])
    landed(codes_out, back_sems.at[0])
    landed(scales_out, back_sems.at[1])


def unpack(codes, scales, surface, tracer_out, surface_out):
    for u in range(codes.shape[0]):
        values = decode(codes[u])
        for a in range(2):
            tracer_out[a, u] = values[a] * scales[pl.ds(a, 1), :]
    surface_out[...] = surface[...]


def local(
    tracer_adjoint,
    surface_adjoint,
    velocity,
    vertical_coupling,
    ocean_levels,
    face_conductance,
    buoyancy_weights,
    surface_flux,
):
    groups, tiles = lax.axis_size("grp"), lax.axis_size("tile")
    levels = vertical_coupling.shape[0]
    share = levels // tiles
    cells = (ROWS, LANES)
    blocks = 2 * UP + 1
    f32, i32 = jnp.float32, jnp.int32
    vmem = pl.BlockSpec(memory_space=pltpu.VMEM)
    dma = pltpu.SemaphoreType.DMA
    packed = (tiles, share) + cells
    quads = tiles // QUAD
    row_blocks = (CHUNKS, quads // CHUNKS, 2 * QUAD * share, LANES)
    codes, scales, surface = pl.pallas_call(
        functools.partial(kernel, (groups, tiles, share, levels)),
        out_shape=(
            pltpu.VMEM((share, ROWS, tiles * LANES), i32),
            pltpu.VMEM((2, tiles * LANES), f32),
            pltpu.VMEM(surface_adjoint.shape, f32),
        ),
        in_specs=[pl.BlockSpec(memory_space=pltpu.HBM)] * 8,
        out_specs=(vmem,) * 3,
        scratch_shapes=[
            pltpu.VMEM(tracer_adjoint.shape, f32),
            pltpu.VMEM(cells, f32),
            pltpu.VMEM(vertical_coupling.shape, f32),
            pltpu.VMEM(cells, i32),
            pltpu.VMEM((4,) + cells, f32),
            pltpu.SMEM(buoyancy_weights.shape, f32),
            pltpu.SMEM(surface_flux.shape, f32),
            pltpu.VMEM(packed, i32),
            pltpu.VMEM((tiles, 2, LANES), f32),
            pltpu.VMEM(packed, i32),
            pltpu.VMEM((tiles, 2, LANES), f32),
            pltpu.VMEM((2, levels) + cells, jnp.bfloat16),
            pltpu.VMEM(packed, i32),
            pltpu.VMEM((tiles, 2, LANES), f32),
            pltpu.VMEM((FIELDS,) + cells, f32),
            pltpu.VMEM(cells, f32),
            pltpu.VMEM((blocks - 1, FIELDS) + cells, f32),
            pltpu.VMEM((blocks, 2) + cells, f32),
            pltpu.VMEM((blocks, 3) + cells, f32),
            pltpu.VMEM((FIELDS, HIGH, 2 * LANES), f32),
            pltpu.VMEM((4, HIGH, 2 * LANES), f32),
            pltpu.VMEM((levels,) + cells, f32),
            pltpu.VMEM((levels,) + cells, f32),
            pltpu.VMEM((levels,) + cells, f32),
            pltpu.VMEM((2, levels) + cells, f32),
            pltpu.VMEM((2, levels) + cells, f32),
            pltpu.VMEM(cells, f32),
            pltpu.VMEM((1 + CHUNKS, 2, 2) + cells, f32),
            pltpu.VMEM((1 + CHUNKS, 2, 2) + cells, f32),
            pltpu.VMEM((STEPS, 2) + row_blocks, f32),
            pltpu.VMEM((STEPS, 2) + row_blocks, f32),
            dma((7,)),
            dma((tiles,)),
            dma((tiles,)),
            dma((tiles,)),
            dma((5,)),
            dma((2,)),
            dma((3, 2, blocks)),
            dma((1 + CHUNKS, 2, 2)),
            dma((1 + CHUNKS, 2, 2)),
        ],
        compiler_params=pltpu.CompilerParams(
            collective_id=0, has_side_effects=True, vmem_limit_bytes=24 << 20
        ),
    )(
        *[
            pltpu.with_memory_space_constraint(value, pltpu.HBM)
            for value in (
                tracer_adjoint,
                surface_adjoint,
                velocity,
                vertical_coupling,
                ocean_levels,
                face_conductance,
                buoyancy_weights,
                surface_flux,
            )
        ]
    )
    return pl.pallas_call(
        unpack,
        out_shape=(
            jax.ShapeDtypeStruct(tracer_adjoint.shape, f32),
            jax.ShapeDtypeStruct(surface_adjoint.shape, f32),
        ),
        in_specs=[vmem] * 3,
        out_specs=(vmem, vmem),
        compiler_params=pltpu.CompilerParams(vmem_limit_bytes=8 << 20),
    )(codes, scales, surface)


def solution(mesh):
    in_specs = (
        P(None, "tile", "grp", None),
        P("grp", "tile"),
        P(None, "tile", "grp", None),
        P(None, "grp", "tile"),
        P("grp", "tile"),
        P(None, "grp", "tile"),
        P(),
        P(),
    )
    out_specs = (P(None, "tile", "grp", None), P("grp", "tile"))
    return jax.shard_map(local, mesh=mesh, in_specs=in_specs, out_specs=out_specs, check_vma=False)
```

```python
import functools

import jax
import jax.numpy as jnp
from jax import lax
from jax.experimental import pallas as pl
from jax.experimental.pallas import tpu as pltpu
from jax.sharding import PartitionSpec as P

SOLVE_ITERS = 12
STEPS = 2
DIFFUSION = 0.1
CODE_MAX = 32767.0
MESH = pl.DeviceIdType.MESH
ROWS = 8
LANES = 128
UP = 2
HIGH = (2 * UP + 1) * ROWS
EDGE = 16
FIELDS = 4
QUAD = 4
CHUNKS = 4
EARLY = 8


def wrap(value, size):
    return lax.rem(value + 2 * size, size)


def push(src, dst, send_sem, recv_sem, device):
    return pltpu.make_async_remote_copy(
        src_ref=src,
        dst_ref=dst,
        send_sem=send_sem,
        recv_sem=recv_sem,
        device_id=device,
        device_id_type=MESH,
    )


def landed(ref, sem):
    pltpu.make_async_copy(ref, ref, sem).wait()


def lanes_of(i):
    return pl.ds(pl.multiple_of(i * LANES, LANES), LANES)


def decode(word):
    first = lax.shift_right_arithmetic(word + 32768, 16)
    second = word - lax.shift_left(first, 16)
    return (first.astype(jnp.float32), second.astype(jnp.float32))


def kernel(
    sizes,
    tracer_in,
    surface_in,
    velocity_in,
    coupling_in,
    ocean_levels,
    conductance_in,
    weights_in,
    flux_in,
    codes_out,
    scales_out,
    surface_out,
    tracer,
    velocity,
    surface,
    coupling,
    depths,
    conductance,
    weights,
    flux,
    sent_codes,
    sent_scales,
    codes,
    scales,
    currents,
    back_codes,
    back_scales,
    mine,
    mine_edge,
    middle,
    sides,
    around,
    fields,
    folded,
    inverse,
    lower,
    forward,
    grad,
    partial,
    surf_block,
    lane_send,
    lane_recv,
    row_send,
    row_recv,
    load_sems,
    code_sems,
    scale_sems,
    current_sems,
    send_sems,
    back_sems,
    near_sems,
    lane_sems,
    row_sems,
):
    groups, tiles, share, levels = sizes
    quads = tiles // QUAD
    deep = QUAD * share
    group = lax.axis_index("grp")
    tile = lax.axis_index("tile")
    def near_device(a, b):
        return (group - (a - UP), wrap(tile - (b - 1), tiles))

    above = [(group + a >= 0) & (group + a < groups) for a in range(-UP, UP + 1)]
    below = above[::-1]

    def where_present(present, action):
        for a in range(2 * UP + 1):
            if a == UP:
                action(a)
            else:
                pl.when(present[a])(functools.partial(action, a))

    loads = [
        pltpu.make_async_copy(src, dst, load_sems.at[n])
        for n, (src, dst) in enumerate(
            [
                (tracer_in, tracer),
                (conductance_in, conductance),
                (surface_in, surface),
                (ocean_levels, depths),
                (coupling_in, coupling),
                (weights_in, weights),
                (flux_in, flux),
                (velocity_in, velocity),
            ]
        )
    ]
    loads[7].start()
    loads[0].start()

    barrier = pltpu.get_barrier_semaphore()

    for i in range(1, tiles):
        pl.semaphore_signal(
            barrier, inc=1, device_id=(group, wrap(tile + i, tiles)), device_id_type=MESH
        )

    def greet_rows(a):
        for b in range(3):
            if a != UP:
                pl.semaphore_signal(
                    barrier, inc=1, device_id=near_device(a, b), device_id_type=MESH
                )

    where_present(below, greet_rows)
    for load in loads[1:7]:
        load.start()
    loads[7].wait()

    rows_near = 0
    for a in range(1, UP + 1):
        rows_near += (group + groups - a) // groups + (2 * groups - 1 - group - a) // groups
    pl.semaphore_wait(barrier, tiles - 1 + 3 * rows_near)

    def others(action, first=1, last=tiles):
        def one(i, _):
            action(wrap(tile + i, tiles))
            return 0

        lax.fori_loop(first, last, one, 0)

    def send_current(to):
        push(
            velocity.at[:, :, :, lanes_of(to)],
            currents.at[:, pl.ds(tile * share, share)],
            send_sems.at[0],
            current_sems.at[tile],
            (group, to),
        ).start()

    others(send_current, 1, 1 + EARLY)
    pltpu.make_async_copy(
        velocity.at[:, :, :, lanes_of(tile)],
        currents.at[:, pl.ds(tile * share, share)],
        current_sems.at[tile],
    ).start()

    lane = lax.broadcasted_iota(jnp.int32, (ROWS, LANES), 1)
    row = lax.broadcasted_iota(jnp.int32, (ROWS, LANES), 0)
    loads[1].wait()
    loads[2].wait()
    own = [
        conductance[0],
        conductance[2],
        1.0 / (1.0 + conductance[0] + conductance[1] + conductance[2] + conductance[3]),
        surface[...],
    ]
    packed = own[0]
    for f in range(FIELDS):
        mine[f] = own[f]
        western = own[f] if f == 0 else pltpu.roll(own[f], EDGE * f, 1)
        eastern = pltpu.roll(own[f], LANES // 2 + EDGE * (f + 1), 1)
        packed = jnp.where((lane >= EDGE * f) & (lane < EDGE * (f + 1)), western, packed)
        packed = jnp.where(
            (lane >= LANES // 2 + EDGE * f) & (lane < LANES // 2 + EDGE * (f + 1)), eastern, packed
        )
    mine_edge[...] = packed

    def encode(values, slot, code_ref, scale_ref):
        rounded = []
        for a in range(2):
            peak = functools.reduce(jnp.maximum, [jnp.abs(v) for v in values[a]])
            peak = jnp.maximum(jnp.max(peak, axis=0, keepdims=True), 1e-30)
            gain = jnp.broadcast_to(CODE_MAX / peak, (ROWS, LANES))
            scale_ref[slot, pl.ds(a, 1), :] = peak * (1.0 / CODE_MAX)
            rounded.append([jnp.floor(v * gain + 0.5).astype(jnp.int32) for v in values[a]])
        for u in range(share):
            code_ref[slot, u] = lax.shift_left(rounded[0][u], 16) + rounded[1][u]

    loads[0].wait()

    def encode_tracer(to, _):
        values = [[tracer[a, u, :, lanes_of(to)] for u in range(share)] for a in range(2)]
        encode(values, to, sent_codes, sent_scales)
        return 0

    lax.fori_loop(0, tiles, encode_tracer, 0)

    def middle_slot(a):
        return a if a < UP else a - 1

    def send_fields(a):
        for b in range(3):
            if b != 1:
                push(
                    mine_edge,
                    sides.at[a, b // 2],
                    near_sems.at[1, 0, a],
                    near_sems.at[1, 1, a],
                    near_device(a, b),
                ).start()
            elif a != UP:
                push(
                    mine,
                    middle.at[middle_slot(a)],
                    near_sems.at[0, 0, a],
                    near_sems.at[0, 1, a],
                    near_device(a, b),
                ).start()

    def fields_passed(a, way):
        landed(sides.at[a], near_sems.at[1, way, a])
        if a != UP:
            landed(middle.at[middle_slot(a)], near_sems.at[0, way, a])

    def send_around(a):
        for b in range(3):
            if (a, b) != (UP, 1):
                push(
                    surf_block,
                    around.at[a, b],
                    near_sems.at[2, 0, a],
                    near_sems.at[2, 1, a],
                    near_device(a, b),
                ).start()

    def around_passed(a, way):
        blocks = around.at[a, pl.ds(0, 2)] if a == UP else around.at[a]
        landed(blocks, near_sems.at[2, way, a])

    where_present(below, send_fields)

    def send_codes(to):
        push(
            sent_codes.at[to], codes.at[tile], send_sems.at[1], code_sems.at[tile], (group, to)
        ).start()
        push(
            sent_scales.at[to], scales.at[tile], send_sems.at[2], scale_sems.at[tile], (group, to)
        ).start()

    others(send_codes)
    pltpu.make_async_copy(sent_codes.at[tile], codes.at[tile], code_sems.at[tile]).start()
    pltpu.make_async_copy(sent_scales.at[tile], scales.at[tile], scale_sems.at[tile]).start()
    others(send_current, 1 + EARLY, tiles)
    for load in loads[3:7]:
        load.wait()
    depth = depths[...]

    def factor(k, carry):
        previous, level_coup = carry
        following = jnp.where(k + 1 < depth, coupling[jnp.minimum(k + 1, levels - 1)], 0.0)
        diagonal = 1.0 + level_coup + following
        reciprocal = 1.0 / (diagonal - level_coup * previous)
        ahead = following * reciprocal
        inverse[k] = reciprocal
        lower[k] = level_coup * reciprocal
        forward[k] = ahead
        return (ahead, following)

    nothing = jnp.zeros((ROWS, LANES), jnp.float32)
    lax.fori_loop(0, levels, factor, (nothing, nothing))

    east_lanes = lane < EDGE
    side_inside = (east_lanes & (tile < tiles - 1)) | ((lane >= LANES - EDGE) & (tile > 0))

    def place(f, a, middle_block, side_block):
        rows = pl.ds(a * ROWS, ROWS)
        fields[f, rows, pl.ds(0, LANES)] = jnp.where(above[a], middle_block, 0.0)
        fields[f, rows, pl.ds(LANES, LANES)] = jnp.where(
            side_inside & above[a], side_block, 0.0
        )

    where_present(above, lambda a: fields_passed(a, 1))
    for a in range(2 * UP + 1):
        from_west, from_east = sides[a, 0], sides[a, 1]
        for f in range(FIELDS):
            east = from_east if f == 0 else pltpu.roll(from_east, LANES - EDGE * f, 1)
            west = pltpu.roll(from_west, (LANES // 2 - EDGE * (f + 1)) % LANES, 1)
            place(
                f,
                a,
                mine[f] if a == UP else middle[middle_slot(a), f],
                jnp.where(east_lanes, east, west),
            )
    eastern, northern, region_recip = fields[0], fields[1], fields[2]
    folded[0] = eastern * region_recip
    folded[1] = pltpu.roll(eastern, 1, 1) * region_recip
    folded[2] = northern * region_recip
    folded[3] = pltpu.roll(northern, 1, 0) * region_recip

    def relax():
        source = fields[FIELDS - 1]
        scaled = source * fields[2]

        def sweep(_, iterate):
            return (
                scaled
                + folded[0] * pltpu.roll(iterate, 2 * LANES - 1, 1)
                + folded[1] * pltpu.roll(iterate, 1, 1)
                + folded[2] * pltpu.roll(iterate, HIGH - 1, 0)
                + folded[3] * pltpu.roll(iterate, 1, 0)
            )

        solved = lax.fori_loop(0, SOLVE_ITERS, sweep, source)
        return solved[UP * ROWS : (UP + 1) * ROWS, :LANES]

    def downward(k, sources, relaxed, carry):
        wet = jnp.where(k < depth, relaxed, 0.0)
        level_inv, level_low = inverse[k], lower[k]
        done = []
        for a in range(2):
            current = (sources[a] + weights[a, k] * wet) * level_inv + level_low * carry[a]
            grad[a, k] = current
            done.append(current)
        return tuple(done)

    def upward():
        def rise(j, carry):
            for u in range(deep):
                k = levels - 1 - (j * deep + u)
                ahead = forward[k]
                wet = k < depth
                carry = tuple(grad[a, k] + ahead * carry[a] for a in range(2))
                for a in range(2):
                    grad[a, k] = jnp.where(wet, carry[a], 0.0)
            return carry

        return lax.fori_loop(0, quads, rise, (nothing, nothing))

    def next_surface(relaxed, top):
        return relaxed + jnp.where(0 < depth, flux[0] * top[0] + flux[1] * top[1], 0.0)

    def row_place(quad):
        return (lax.rem(quad, CHUNKS), lax.div(quad, CHUNKS))

    southern, northern = group > 0, group < groups - 1

    def send_rows(step, message, quad, ready=None):
        chunk, half = row_place(quad)
        for side, present in enumerate((southern, northern)):
            copy = push(
                row_send.at[step, side, chunk, half],
                row_recv.at[step, side, chunk, half],
                row_sems.at[message, 0, side],
                row_sems.at[message, 1, side],
                (group - 1 + 2 * side, tile),
            )
            pl.when(present if ready is None else present & ready)(copy.start)

    def give(step, quad, carry):
        carry = list(carry)
        chunk, half = row_place(quad)
        for u in range(deep):
            k = quad * deep + u
            zonal = 0.5 * currents[0, k].astype(jnp.float32)
            meridional = 0.5 * currents[1, k].astype(jnp.float32)
            for a in range(2):
                masked = grad[a, k]
                westward = masked * (DIFFUSION + zonal)
                eastward = masked * (DIFFUSION - zonal)
                southward = masked * (DIFFUSION + meridional)
                northward = pltpu.roll(masked * (DIFFUSION - meridional), 1, 0)
                partial[a, k] = (
                    (1.0 - 4.0 * DIFFUSION) * masked
                    + jnp.where(lane == LANES - 1, 0.0, pltpu.roll(westward, LANES - 1, 1))
                    + jnp.where(lane == 0, 0.0, pltpu.roll(eastward, 1, 1))
                    + jnp.where(row == ROWS - 1, 0.0, pltpu.roll(southward, ROWS - 1, 0))
                    + jnp.where(row == 0, 0.0, northward)
                )
                at_level = lane == k
                carry[2 * a] = jnp.where(at_level, pltpu.roll(westward, k, 1), carry[2 * a])
                carry[2 * a + 1] = jnp.where(
                    at_level, pltpu.roll(eastward, k + 1, 1), carry[2 * a + 1]
                )
                at_row = pl.ds(a * deep + u, 1)
                row_send[step, 0, chunk, half, at_row, :] = southward[0:1]
                row_send[step, 1, chunk, half, at_row, :] = northward[0:1]
        return tuple(carry)

    def keep_edges(message, edges):
        for a in range(2):
            for side in range(2):
                lane_send[message, side, a] = edges[2 * a + side]

    def lane_copies(message):
        return [
            push(
                lane_send.at[message, side],
                lane_recv.at[message, side],
                lane_sems.at[message, 0, side],
                lane_sems.at[message, 1, side],
                (group, wrap(tile - 1 + 2 * side, tiles)),
            )
            for side in range(2)
        ]

    def rows_passed(way, step, message):
        for side in range(2):
            rows = row_recv.at[step, side]
            if step:
                rows = rows.at[message - 1]
            present = (southern, northern)[side if way == 0 else 1 - side]
            pl.when(present)(
                functools.partial(landed, rows, row_sems.at[message, way, side])
            )

    at_east = (lane == LANES - 1) & (tile < tiles - 1)
    at_west = (lane == 0) & (tile > 0)
    at_north = (row == ROWS - 1) & (group < groups - 1)
    at_south = (row == 0) & (group > 0)

    def gathered(step, message, a, quad, u):
        k = quad * deep + u
        chunk, half = row_place(quad)
        at_row = pl.ds(a * deep + u, 1)
        east = pltpu.roll(lane_recv[message, 0, a], LANES - 1 - k, 1)
        west = pltpu.roll(lane_recv[message, 1, a], LANES - k, 1)
        north = row_recv[step, 0, chunk, half, at_row, :]
        south = row_recv[step, 1, chunk, half, at_row, :]
        return (
            partial[a, k]
            + jnp.where(at_east, east, 0.0)
            + jnp.where(at_west, west, 0.0)
            + jnp.where(at_north, jnp.broadcast_to(north, (ROWS, LANES)), 0.0)
            + jnp.where(at_south, jnp.broadcast_to(south, (ROWS, LANES)), 0.0)
        )

    relaxed = relax()

    def first_down(s, carry):
        landed(codes.at[s], code_sems.at[s])
        landed(scales.at[s], scale_sems.at[s])
        factors = [scales[s, pl.ds(a, 1), :] for a in range(2)]
        for u in range(share):
            k = s * share + u
            values = decode(codes[s, u])
            carry = downward(k, [values[a] * factors[a] for a in range(2)], relaxed, carry)
        return carry

    lax.fori_loop(0, tiles, first_down, (nothing, nothing))
    top = upward()
    surf_block[...] = next_surface(relaxed, top)

    def arrived_quad(i):
        return wrap(lax.div(tile, QUAD) - i, quads)

    def arrived_give(i, carry):
        quad = arrived_quad(i)
        for v in range(QUAD):
            s = quad * QUAD + v
            landed(currents.at[:, pl.ds(s * share, share)], current_sems.at[s])
        return give(0, quad, carry)

    edges = arrived_give(0, (nothing,) * 4)
    where_present(below, send_around)

    def send_and_give(i, carry):
        send_rows(0, 0, arrived_quad(i - 1))
        return arrived_give(i, carry)

    edges = lax.fori_loop(1, quads, send_and_give, edges)
    keep_edges(0, edges)
    send_rows(0, 0, arrived_quad(quads - 1))

    for copy in lane_copies(0):
        copy.start()
    where_present(above, lambda a: around_passed(a, 1))
    for a in range(2 * UP + 1):
        blocks = [surf_block if (a, b) == (UP, 1) else around.at[a, b] for b in range(3)]
        place(FIELDS - 1, a, blocks[1][...], jnp.where(east_lanes, blocks[2][...], blocks[0][...]))
    relaxed_again = relax()
    for copy in lane_copies(0):
        copy.wait_recv()
    rows_passed(1, 0, 0)

    def second_down(quad, carry):
        for u in range(deep):
            sources = [gathered(0, 0, a, quad, u) for a in range(2)]
            carry = downward(quad * deep + u, sources, relaxed_again, carry)
        return carry

    lax.fori_loop(0, quads, second_down, (nothing, nothing))
    top = upward()
    surface_out[...] = next_surface(relaxed_again, top)

    turn = lax.div(lax.div(tile, QUAD), CHUNKS)

    def quad_of(chunk, i):
        return wrap(turn - i, quads // CHUNKS) * CHUNKS + chunk

    for chunk in range(CHUNKS):

        def give_and_send(i, carry, chunk=chunk):
            send_rows(1, 1 + chunk, quad_of(chunk, i - 1), i > 0)
            return give(1, quad_of(chunk, i), carry)

        edges = lax.fori_loop(0, quads // CHUNKS, give_and_send, (nothing,) * 4)
        keep_edges(1 + chunk, edges)
        send_rows(1, 1 + chunk, quad_of(chunk, quads // CHUNKS - 1))
        for copy in lane_copies(1 + chunk):
            copy.start()

    landed(currents.at[:, pl.ds(0, levels - share)], send_sems.at[0])
    landed(sent_codes.at[pl.ds(0, tiles - 1)], send_sems.at[1])
    landed(sent_scales.at[pl.ds(0, tiles - 1)], send_sems.at[2])

    def near_sent(a):
        fields_passed(a, 0)
        around_passed(a, 0)

    where_present(below, near_sent)
    for copy in lane_copies(0):
        copy.wait_send()
    rows_passed(0, 0, 0)

    def back_refs(to):
        return [
            (back_codes.at[to], codes_out.at[:, :, lanes_of(tile)], 0),
            (back_scales.at[to], scales_out.at[:, lanes_of(tile)], 1),
        ]

    def send_back(quad):
        for v in range(QUAD):
            to = quad * QUAD + v

            @pl.when(to != tile)
            def _():
                for src, dst, n in back_refs(to):
                    push(src, dst, send_sems.at[3 + n], back_sems.at[n], (group, to)).start()

    for chunk in range(CHUNKS):
        for copy in lane_copies(1 + chunk):
            copy.wait_recv()
        rows_passed(1, 1, 1 + chunk)

        def finish(i, _, chunk=chunk):
            quad = quad_of(chunk, i)
            for v in range(QUAD):
                values = [
                    [gathered(1, 1 + chunk, a, quad, v * share + u) for u in range(share)]
                    for a in range(2)
                ]
                encode(values, quad * QUAD + v, back_codes, back_scales)

            @pl.when(i > 0)
            def _():
                send_back(quad_of(chunk, i - 1))

            return 0

        lax.fori_loop(0, quads // CHUNKS, finish, 0)
        send_back(quad_of(chunk, quads // CHUNKS - 1))
    for src, dst, n in back_refs(tile):
        pltpu.make_async_copy(src, dst, back_sems.at[n]).start()

    for chunk in range(CHUNKS):
        for copy in lane_copies(1 + chunk):
            copy.wait_send()
        rows_passed(0, 1, 1 + chunk)
    landed(back_codes.at[pl.ds(0, tiles - 1)], send_sems.at[3])
    landed(back_scales.at[pl.ds(0, tiles - 1)], send_sems.at[4])
    landed(codes_out, back_sems.at[0])
    landed(scales_out, back_sems.at[1])


def unpack(codes, scales, surface, tracer_out, surface_out):
    for u in range(codes.shape[0]):
        values = decode(codes[u])
        for a in range(2):
            tracer_out[a, u] = values[a] * scales[pl.ds(a, 1), :]
    surface_out[...] = surface[...]


def local(
    tracer_adjoint,
    surface_adjoint,
    velocity,
    vertical_coupling,
    ocean_levels,
    face_conductance,
    buoyancy_weights,
    surface_flux,
):
    groups, tiles = lax.axis_size("grp"), lax.axis_size("tile")
    levels = vertical_coupling.shape[0]
    share = levels // tiles
    cells = (ROWS, LANES)
    blocks = 2 * UP + 1
    f32, i32 = jnp.float32, jnp.int32
    vmem = pl.BlockSpec(memory_space=pltpu.VMEM)
    dma = pltpu.SemaphoreType.DMA
    packed = (tiles, share) + cells
    quads = tiles // QUAD
    row_blocks = (CHUNKS, quads // CHUNKS, 2 * QUAD * share, LANES)
    codes, scales, surface = pl.pallas_call(
        functools.partial(kernel, (groups, tiles, share, levels)),
        out_shape=(
            pltpu.VMEM((share, ROWS, tiles * LANES), i32),
            pltpu.VMEM((2, tiles * LANES), f32),
            pltpu.VMEM(surface_adjoint.shape, f32),
        ),
        in_specs=[pl.BlockSpec(memory_space=pltpu.HBM)] * 8,
        out_specs=(vmem,) * 3,
        scratch_shapes=[
            pltpu.VMEM(tracer_adjoint.shape, f32),
            pltpu.VMEM(velocity.shape, velocity.dtype),
            pltpu.VMEM(cells, f32),
            pltpu.VMEM(vertical_coupling.shape, f32),
            pltpu.VMEM(cells, i32),
            pltpu.VMEM((4,) + cells, f32),
            pltpu.SMEM(buoyancy_weights.shape, f32),
            pltpu.SMEM(surface_flux.shape, f32),
            pltpu.VMEM(packed, i32),
            pltpu.VMEM((tiles, 2, LANES), f32),
            pltpu.VMEM(packed, i32),
            pltpu.VMEM((tiles, 2, LANES), f32),
            pltpu.VMEM((2, levels) + cells, jnp.bfloat16),
            pltpu.VMEM(packed, i32),
            pltpu.VMEM((tiles, 2, LANES), f32),
            pltpu.VMEM((FIELDS,) + cells, f32),
            pltpu.VMEM(cells, f32),
            pltpu.VMEM((blocks - 1, FIELDS) + cells, f32),
            pltpu.VMEM((blocks, 2) + cells, f32),
            pltpu.VMEM((blocks, 3) + cells, f32),
            pltpu.VMEM((FIELDS, HIGH, 2 * LANES), f32),
            pltpu.VMEM((4, HIGH, 2 * LANES), f32),
            pltpu.VMEM((levels,) + cells, f32),
            pltpu.VMEM((levels,) + cells, f32),
            pltpu.VMEM((levels,) + cells, f32),
            pltpu.VMEM((2, levels) + cells, f32),
            pltpu.VMEM((2, levels) + cells, f32),
            pltpu.VMEM(cells, f32),
            pltpu.VMEM((1 + CHUNKS, 2, 2) + cells, f32),
            pltpu.VMEM((1 + CHUNKS, 2, 2) + cells, f32),
            pltpu.VMEM((STEPS, 2) + row_blocks, f32),
            pltpu.VMEM((STEPS, 2) + row_blocks, f32),
            dma((8,)),
            dma((tiles,)),
            dma((tiles,)),
            dma((tiles,)),
            dma((5,)),
            dma((2,)),
            dma((3, 2, blocks)),
            dma((1 + CHUNKS, 2, 2)),
            dma((1 + CHUNKS, 2, 2)),
        ],
        compiler_params=pltpu.CompilerParams(
            collective_id=0, has_side_effects=True, vmem_limit_bytes=24 << 20
        ),
    )(
        *[
            pltpu.with_memory_space_constraint(value, pltpu.HBM)
            for value in (
                tracer_adjoint,
                surface_adjoint,
                velocity,
                vertical_coupling,
                ocean_levels,
                face_conductance,
                buoyancy_weights,
                surface_flux,
            )
        ]
    )
    return pl.pallas_call(
        unpack,
        out_shape=(
            jax.ShapeDtypeStruct(tracer_adjoint.shape, f32),
            jax.ShapeDtypeStruct(surface_adjoint.shape, f32),
        ),
        in_specs=[vmem] * 3,
        out_specs=(vmem, vmem),
        compiler_params=pltpu.CompilerParams(vmem_limit_bytes=8 << 20),
    )(codes, scales, surface)


def solution(mesh):
    in_specs = (
        P(None, "tile", "grp", None),
        P("grp", "tile"),
        P(None, "tile", "grp", None),
        P(None, "grp", "tile"),
        P("grp", "tile"),
        P(None, "grp", "tile"),
        P(),
        P(),
    )
    out_specs = (P(None, "tile", "grp", None), P("grp", "tile"))
    return jax.shard_map(local, mesh=mesh, in_specs=in_specs, out_specs=out_specs, check_vma=False)
```
